128 devices in a mesh: grp: 4 (over x), dev: 32 (over y, z, core).
Axes of the slice: x: 4, y: 4, z: 4, core: 2. Of those that a mesh axis runs over, the one named last changes fastest.
Arguments:
- canvas: bfloat16 [256, 4096, 256], P('grp', 'dev'), may hold values from -6 to 6
- conv_weight: bfloat16 [2304, 256], replicated, may hold values from -0.125 to 0.125
- conv_bias: float32 [256], replicated, may hold values from -3 to 3
- score_weight: float32 [256], replicated, may hold values from -0.75 to 0.75
- tile_tokens: bfloat16 [4096, 24, 3200], P(('grp', 'dev')), may hold values from -6 to 6
- tile_cell: int32 [4, 1024], P('grp', 'dev'), may hold values from 0 to 8191
- tile_count: int32 [4, 32], P('grp'), may hold values from 1 to 32, 256 in all within a row
- holder_order: int32 [4, 32], P('grp'), may hold values from 0 to 31, each once within a row
- tile_image: int32 [4, 256], P('grp'), may hold values from 0 to 127, never falling along the last dimension, each value on 1 to 9 neighbouring positions
- ln_gain: float32 [3200], replicated, may hold values from 0.25 to 1.75
- qkv_weight: bfloat16 [3200, 4992], P(('grp', 'dev')), may hold values from -2 to 2
Outputs:
- score_map: float32 [256, 4096], P('grp', 'dev')
- attended: bfloat16 [24576, 1664], P(('grp', 'dev'))
The draws below stay inside these ranges and needn't reach their ends.
Inputs may be any that keep to these rules, and one draw needn't show every extreme that they name: `tile_count`: the counts of one group add up to 256; in each group one device holds exactly 32. `tile_image`: ids never fall along a group's held tiles; each image has 1 to 9 tiles and one has exactly 9.
All inputs are finite; a program needn't handle non-finite values.
Results may differ from the reference program's by a relative error of at most 0.012.
Values may be sent and summed in bfloat16 or wider, within the bound.
No kernel may reach another device: no remote copies, remote signals or barrier semaphores. Data moves between devices by JAX's collectives and lax.ppermute only.
A program may use at most 192 MiB of HBM per device.

```python
import math
import jax
import jax.numpy as jnp
import numpy as np
from jax import lax

D = 3200
HD = 128
HEADS = 13
CIN = 256
CHID = 256
CH = 64
CW = 128
TT = 24
MT = 8
SLOTS = 32
HW = 1664
IMAGES = 128
CANVAS_H = 256
CANVAS_W = 4096
TILES = 4096
N_GRP = 4
N_DEV = 32


def draw_tile_tokens(key, part):
    shape = (TILES, TT, D)
    values = jnp.clip(jax.random.normal(key, shape, jnp.float32), -6.0, 6.0)
    return values.astype(jnp.bfloat16)


def draw_qkv_weight(key, part):
    scale = 1.0 / math.sqrt(D)
    whole = jnp.clip(jax.random.normal(key, (D, 3 * HW), jnp.float32), -6.0, 6.0) * scale
    return whole.astype(jnp.bfloat16)


def with_ends(values, key, smallest, largest):
    shape = values.shape
    index_at = [jax.random.randint(jax.random.fold_in(key, axis), (), 0, shape[axis]) for axis in range(len(shape))]
    values = values.at[tuple(index_at)].set(smallest)
    longest = shape.index(max(shape))
    index_at[longest] = (index_at[longest] + 1) % shape[longest]
    return values.at[tuple(index_at)].set(largest)


def block_scale(key, shape, shards, low, high):
    level, own = 1.0, jax.random.fold_in(key, 6)
    for dim, shards_of in shards:
        draws = jnp.exp(jax.random.uniform(jax.random.fold_in(own, dim), (shards_of,), jnp.float32, low / len(shards), high / len(shards)))
        level = level * jnp.repeat(draws, shape[dim] // shards_of).reshape([-1 if axis == dim else 1 for axis in range(len(shape))])
    return level


def split_up(number_of, total, reach, skew):
    weights = [(1 << 20) // math.isqrt(grade ** skew) + 1 for grade in range(2, number_of + 1)]
    spare, given = total - reach - (number_of - 1), [1] * (number_of - 1)
    while spare > 0:
        movable = [i for i in range(number_of - 1) if given[i] < reach]
        whole, budget = sum([weights[i] for i in movable]), spare
        for i in movable:
            more = min(reach - given[i], max(1, budget * weights[i] // whole), spare)
            given[i] = given[i] + more
            spare = spare - more
    return np.array([reach] + given)


def uneven_parts(rng, number_of, total, most, skew):
    if number_of == 2:
        one = jax.random.randint(rng, (), max(1, total - most), min(most, total - 1) + 1)
        return jnp.stack([one, total - one])
    lengths = jnp.asarray(split_up(number_of, total, most, skew), jnp.int32)
    pairs = (number_of - 1) // 2
    giver, taker = lengths[1:1 + 2 * pairs:2], lengths[2:2 + 2 * pairs:2]
    slack = jnp.minimum(giver - 1, most - taker)
    passed = jax.random.randint(jax.random.fold_in(rng, 1), (pairs,), 0, 1 << 20) % (slack + 1)
    lengths = lengths.at[1:1 + 2 * pairs:2].set(giver - passed).at[2:2 + 2 * pairs:2].set(taker + passed)
    return lengths[jax.random.permutation(jax.random.fold_in(rng, 2), number_of)]


def scatter_about(key, extent, deviation, limit, cuts=(), held_as=jnp.bfloat16):
    drawn = deviation * jax.random.normal(key, extent, jnp.float32)
    if cuts:
        drawn = drawn * block_scale(key, extent, cuts, -0.22, 0.18)
    return jnp.clip(drawn, -limit, limit).astype(held_as)


def setup_inputs(seed: int = 0) -> dict:
    key_list = jax.random.split(jax.random.key(seed), 12)
    canvas = scatter_about(key_list[0], (CANVAS_H, CANVAS_W, CIN), 1.0, 6.0, ((0, 4), (1, 32)))
    conv_weight = scatter_about(key_list[1], (9 * CIN, CHID), (9 * CIN) ** -0.5, 0.125)
    conv_bias = scatter_about(key_list[2], (CHID,), 0.5, 3.0, (), jnp.float32)
    score_weight = scatter_about(key_list[3], (CHID,), (CHID // 4) ** -0.5, 0.75, (), jnp.float32)
    tile_tokens = draw_tile_tokens(jax.random.fold_in(key_list[11], 71), 0)
    tile_cell = with_ends(jax.random.randint(key_list[5], (N_GRP, N_DEV * SLOTS), 0, CH * CW), jax.random.fold_in(key_list[5], 1), 0, (CH * CW) - 1).astype(jnp.int32)
    tile_count = jax.vmap(lambda own: uneven_parts(own, N_DEV, MT * N_DEV, SLOTS, 2))(jax.random.split(key_list[6], N_GRP)).reshape((N_GRP, N_DEV)).astype(jnp.int32)
    holder_order = jax.vmap(lambda own: jax.random.permutation(own, N_DEV))(jax.random.split(key_list[7], N_GRP)).reshape((N_GRP, N_DEV)).astype(jnp.int32)
    tile_image = jax.vmap(lambda own: jnp.searchsorted(jnp.cumsum(uneven_parts(own, IMAGES, N_DEV * MT, MT + 1, 0)), jnp.arange(N_DEV * MT), side="right"))(jax.random.split(key_list[8], N_GRP)).reshape((N_GRP, N_DEV * MT)).astype(jnp.int32)
    ln_gain = jnp.clip(1.0 + 0.15 * jax.random.normal(key_list[9], (D,), jnp.float32), 0.25, 1.75)
    qkv_weight = draw_qkv_weight(jax.random.fold_in(key_list[11], 71), 0)
    return {"canvas": canvas, "conv_weight": conv_weight, "conv_bias": conv_bias, "score_weight": score_weight, "tile_tokens": tile_tokens, "tile_cell": tile_cell, "tile_count": tile_count, "holder_order": holder_order, "tile_image": tile_image, "ln_gain": ln_gain, "qkv_weight": qkv_weight}


def layer_norm(rows, gain):
    values = rows.astype(jnp.float32)
    center = lax.optimization_barrier(jnp.mean(values, axis=1, keepdims=True))
    spread = lax.optimization_barrier(jnp.mean(jnp.square(values - center), axis=1, keepdims=True))
    return ((values - center) * lax.rsqrt(spread + 1e-06) * gain).astype(jnp.bfloat16)

def conv_scores(padded, conv_weight, conv_bias, score_weight, height, breadth):
    channels = padded.shape[2]
    summed = jnp.zeros((height * breadth, conv_weight.shape[1]), jnp.float32)
    for row_off in range(3):
        for col_off in range(3):
            window = padded[row_off:row_off + height, col_off:col_off + breadth].reshape(height * breadth, channels)
            offset = (row_off * 3 + col_off) * channels
            summed = summed + jnp.dot(window, conv_weight[offset:offset + channels], preferred_element_type=jnp.float32)
    hidden = jax.nn.gelu(summed + conv_bias)
    return jnp.dot(hidden, score_weight, precision=lax.Precision.HIGHEST)

def attend(queries, keys, values, query_ids, key_ids):
    rows = queries.shape[0]
    query_heads = queries.astype(jnp.float32).reshape(rows, HEADS, HD)
    key_heads = keys.astype(jnp.float32).reshape(keys.shape[0], HEADS, HD)
    value_heads = values.astype(jnp.float32).reshape(values.shape[0], HEADS, HD)
    logits = jnp.einsum('qhd,khd->hqk', query_heads, key_heads, precision=lax.Precision.HIGHEST) * (1.0 / math.sqrt(HD))
    same = query_ids[:, None] == key_ids[None, :]
    logits = jnp.where(same[None], logits, -1e+30)
    peak = lax.optimization_barrier(jnp.max(logits, axis=2, keepdims=True))
    weights = jnp.exp(logits - peak)
    probs = (weights / lax.optimization_barrier(jnp.sum(weights, axis=2, keepdims=True))).astype(jnp.bfloat16)
    result = jnp.einsum('hqk,khd->qhd', probs.astype(jnp.float32), value_heads, precision=lax.Precision.HIGHEST)
    return result.astype(jnp.bfloat16).reshape(rows, HEADS * HD)

def attend_near(queries, keys, values, token_ids, block_rows):
    keys_pad = jnp.pad(keys, ((block_rows, block_rows), (0, 0)))
    values_pad = jnp.pad(values, ((block_rows, block_rows), (0, 0)))
    ids_pad = jnp.pad(token_ids, (block_rows, block_rows), constant_values=-1)
    holder_total = queries.shape[0] // block_rows

    def one_holder(index):
        start = (index * block_rows).astype(jnp.int32)
        own_queries = lax.dynamic_slice_in_dim(queries, start, block_rows, 0)
        near_keys = lax.dynamic_slice_in_dim(keys_pad, start, 3 * block_rows, 0)
        near_values = lax.dynamic_slice_in_dim(values_pad, start, 3 * block_rows, 0)
        own_ids = lax.dynamic_slice_in_dim(token_ids, start, block_rows, 0)
        near_ids = lax.dynamic_slice_in_dim(ids_pad, start, 3 * block_rows, 0)
        return attend(own_queries, near_keys, near_values, own_ids, near_ids)
    outputs = lax.map(one_holder, jnp.arange(holder_total, dtype=jnp.int32))
    return outputs.reshape(queries.shape[0], HW)

def reference(canvas, conv_weight, conv_bias, score_weight, tile_tokens, tile_cell, tile_count, holder_order, tile_image, ln_gain, qkv_weight):
    padded = jnp.pad(canvas, ((1, 1), (1, 1), (0, 0)))
    bands = []
    for group in range(N_GRP):
        band = padded[group * CH:group * CH + CH + 2]
        bands.append(conv_scores(band, conv_weight, conv_bias, score_weight, CH, CW * N_DEV).reshape(CH, CW * N_DEV))
    score_map = jnp.concatenate(bands, 0)
    outputs = []
    for group in range(N_GRP):
        counts = tile_count[group]
        order = holder_order[group]
        prefix = jnp.cumsum(counts) - counts
        place = jnp.zeros((N_DEV,), jnp.int32).at[order].set(jnp.arange(N_DEV, dtype=jnp.int32))
        position = jnp.arange(MT, dtype=jnp.int32)[None, :] * N_DEV + place[:, None]
        source = lax.optimization_barrier(jnp.sum((prefix[None, None, :] <= position[:, :, None]).astype(jnp.int32), axis=2)) - 1
        slot_index = position - prefix[source]
        flat = ((group * N_DEV + source) * SLOTS + slot_index).astype(jnp.int32)
        tokens = tile_tokens[flat.reshape(-1)].reshape(N_DEV * MT * TT, D)
        cells = tile_cell[group][(source * SLOTS + slot_index).astype(jnp.int32)]
        score_rows = (group * CH + cells // CW).astype(jnp.int32)
        score_cols = (source * CW + cells % CW).astype(jnp.int32)
        rounded = lax.optimization_barrier(score_map[score_rows, score_cols].astype(jnp.bfloat16))
        sharpness = 0.5 + jax.nn.softplus(rounded.astype(jnp.float32))
        sharpness = jnp.repeat(sharpness.reshape(-1), TT)
        normed = layer_norm(tokens, ln_gain)
        mixed = jnp.dot(normed, qkv_weight, preferred_element_type=jnp.float32)
        queries = mixed[:, :HW].astype(jnp.bfloat16)
        keys = (mixed[:, HW:2 * HW] * sharpness[:, None]).astype(jnp.bfloat16)
        values = mixed[:, 2 * HW:].astype(jnp.bfloat16)
        token_ids = jnp.repeat(tile_image[group], TT).astype(jnp.int32)
        outputs.append(attend_near(queries, keys, values, token_ids, MT * TT))
    return (score_map, jnp.concatenate(outputs, 0))
```

```python
import math

import jax
import jax.numpy as jnp
import numpy as np
from jax import lax
from jax.experimental import pallas as pl
from jax.experimental.pallas import tpu as pltpu
from jax.sharding import PartitionSpec as P


HD = 128
HEADS = 13
HW = HEADS * HD
MT = 8
BF = jnp.bfloat16
F32 = jnp.float32
ANY = pl.BlockSpec(memory_space=pl.ANY)
SMEM = pl.BlockSpec(memory_space=pltpu.SMEM)
VMEM = pl.BlockSpec(memory_space=pltpu.VMEM)


def ring_pairs(axis):
    size = lax.axis_size(axis)
    up = [(i, i + 1) for i in range(size - 1)]
    return up, [(j, i) for i, j in up]


def send_order(counts, order, own, tokens):
    holders = order.shape[0]

    def body(counts_ref, order_ref, own_ref, tok_ref, out_ref, tiles, in_sems, out_sems):
        fetch = [pltpu.make_async_copy(tok_ref.at[s], tiles.at[s], in_sems.at[s]) for s in range(holders)]
        for c in fetch:
            c.start()
        first = lax.fori_loop(0, own_ref[0], lambda j, acc: acc + counts_ref[j], jnp.int32(0))

        def copy(s):
            holder = order_ref[(first + s) & (holders - 1)]
            return pltpu.make_async_copy(tiles.at[s], out_ref.at[holder], out_sems.at[s])

        for s in range(holders):
            fetch[s].wait()
            copy(s).start()
        for s in range(holders):
            copy(s).wait()

    return pl.pallas_call(
        body,
        out_shape=jax.ShapeDtypeStruct(tokens.shape, tokens.dtype),
        in_specs=[SMEM, SMEM, SMEM, ANY],
        out_specs=ANY,
        scratch_shapes=[
            pltpu.VMEM(tokens.shape, tokens.dtype),
            pltpu.SemaphoreType.DMA((holders,)),
            pltpu.SemaphoreType.DMA((holders,)),
        ],
        name="send_order",
    )(counts, order, own, tokens)


def spread_index(parts, rows):
    part, row = np.arange(parts)[:, None], np.arange(8)[None, :]
    main = [(rows * part + 8 * b + row).reshape(-1) for b in range(rows // 8)]
    return np.concatenate(main + [rows * np.arange(parts) + rows - 1]).astype(np.int32)


def hold_and_norm(source, recv, gain, parts):
    tile_len, width = recv.shape[1], recv.shape[2]
    rows = MT * tile_len
    index = spread_index(parts, width // parts)
    blocks = width // 128
    table = jnp.asarray(index.reshape(blocks, 128))

    def body(src_ref, recv_ref, gain_ref, table_ref, out_ref, tiles, normed, sems):
        copies = [
            pltpu.make_async_copy(recv_ref.at[src_ref[m]], tiles.at[m], sems.at[m]) for m in range(MT)
        ]
        for c in copies:
            c.start()
        for m in range(MT):
            copies[m].wait()
            values = tiles[m].astype(F32)
            center = jnp.mean(values, axis=1, keepdims=True)
            values = values - center
            spread = jnp.mean(values * values, axis=1, keepdims=True)
            scaled = values * lax.rsqrt(spread + 1e-06) * gain_ref[...]
            normed[m * tile_len : (m + 1) * tile_len, :] = scaled.astype(BF)
        for n in range(blocks):
            part = index[n * 128 : (n + 1) * 128]
            low = int(part.min()) // 128 * 128
            high = int(part.max()) // 128 * 128 + 128
            place = lax.broadcasted_iota(jnp.int32, (high - low, 128), 0) + low
            pick = jnp.where(place == table_ref[n : n + 1, :], 1.0, 0.0).astype(BF)
            out_ref[:, n * 128 : (n + 1) * 128] = jnp.dot(
                normed[:, low:high], pick, preferred_element_type=F32
            ).astype(BF)

    return pl.pallas_call(
        body,
        out_shape=jax.ShapeDtypeStruct((rows, width), BF),
        in_specs=[SMEM, ANY, VMEM, VMEM],
        out_specs=VMEM,
        scratch_shapes=[
            pltpu.VMEM((MT, tile_len, width), BF),
            pltpu.VMEM((rows, width), BF),
            pltpu.SemaphoreType.DMA((MT,)),
        ],
        name="hold_and_norm",
    )(source, recv, gain.reshape(1, width), table)


def conv_scores(canvas, top, bottom, left, right, weight, bias, readout):
    height, breadth, channels = canvas.shape
    hidden = weight.shape[1]
    step = 8
    pixels = step * breadth

    def side(edge):
        return jnp.concatenate([edge[0:height], edge[1 : height + 1], edge[2 : height + 2]], axis=1)

    def body(canvas_ref, top_ref, bottom_ref, left_ref, right_ref, w_ref, bias_ref, read_ref, out_ref,
             padded, lside, rside, sem):
        i = pl.program_id(0)

        def w_of(col):
            return jnp.concatenate(
                [w_ref[(row * 3 + col) * channels : (row * 3 + col + 1) * channels, :] for row in range(3)],
                axis=0,
            )

        @pl.when(i == 0)
        def _():
            fetch = pltpu.make_async_copy(canvas_ref, padded.at[pl.ds(1, height)], sem)
            fetch.start()
            padded[0:1] = top_ref[...]
            padded[height + 1 : height + 2] = bottom_ref[...]
            sides = (height // step, step, hidden)
            lside[...] = jnp.dot(left_ref[...], w_of(0), preferred_element_type=F32).reshape(sides)
            rside[...] = jnp.dot(right_ref[...], w_of(2), preferred_element_type=F32).reshape(sides)
            fetch.wait()

        window = jnp.concatenate(
            [padded[pl.ds(i * step + row, step)].reshape(pixels, channels) for row in range(3)], axis=1
        )
        before = jnp.dot(window, w_of(0), preferred_element_type=F32)
        at = jnp.dot(window, w_of(1), preferred_element_type=F32)
        after = jnp.dot(window, w_of(2), preferred_element_type=F32)
        before = pltpu.roll(before, 1, 0).reshape(step, breadth, hidden)
        after = pltpu.roll(after, pixels - 1, 0).reshape(step, breadth, hidden)
        col = lax.broadcasted_iota(jnp.int32, (step, breadth, hidden), 1)
        lrow = lside[i]
        rrow = rside[i]
        before = jnp.where(col == 0, lrow[:, None, :], before)
        after = jnp.where(col == breadth - 1, rrow[:, None, :], after)
        x = (before + after).reshape(pixels, hidden) + at + bias_ref[...]
        inner = math.sqrt(2.0 / math.pi) * (x + 0.044715 * (x * x * x))
        h = x * (0.5 * (1.0 + jnp.tanh(inner)))
        h = h * read_ref[...]
        half = h[:, 0:128]
        for k in range(1, hidden // 128):
            half = half + h[:, k * 128 : (k + 1) * 128]
        ones = jnp.ones((8, 128), F32)
        score = lax.dot_general(
            ones, half, (((1,), (1,)), ((), ())), precision=lax.Precision.HIGHEST, preferred_element_type=F32
        )
        for r in range(step):
            out_ref[0, r : r + 1, :] = score[0:1, r * breadth : (r + 1) * breadth]

    out = pl.pallas_call(
        body,
        grid=(height // step,),
        out_shape=jax.ShapeDtypeStruct((height // step, step, breadth), F32),
        in_specs=[ANY] + [pl.BlockSpec(memory_space=pltpu.VMEM)] * 7,
        out_specs=pl.BlockSpec((1, step, breadth), lambda i: (i, 0, 0)),
        scratch_shapes=[
            pltpu.VMEM((height + 2, breadth, channels), BF),
            pltpu.VMEM((height // step, step, hidden), F32),
            pltpu.VMEM((height // step, step, hidden), F32),
            pltpu.SemaphoreType.DMA,
        ],
        compiler_params=pltpu.CompilerParams(vmem_limit_bytes=32 << 20),
        name="conv_scores",
    )(canvas, top, bottom, side(left), side(right), weight, bias.reshape(1, hidden), readout.reshape(1, hidden))
    return out.reshape(height, breadth)


def pack_rows(weight):
    eights = weight.shape[0] // 8
    tiles = weight.shape[1] // 128
    last = weight[8 * eights :].reshape(tiles, 128)
    last = jnp.pad(last, ((0, -tiles % 8), (0, 0))).reshape(-1, 8, 128)
    pieces = []
    for b in range(eights):
        pieces += [weight[8 * b : 8 * b + 8], last[b]]
    return jnp.concatenate(pieces + [last[j] for j in range(eights, last.shape[0])], axis=1)


def project(normed, packed, sharp, head_width):
    rows, width = normed.shape
    deep = packed.shape[0]
    eights = width // deep
    parts = deep // 8
    pairs = 20
    block = 256

    def body(x_ref, w0, w1, w2, last_ref, sharp_ref, out_ref):
        n = pl.program_id(0)
        acc = jnp.dot(x_ref[:, 0:deep], w0[...], preferred_element_type=F32)
        acc = acc + jnp.dot(x_ref[:, deep : 2 * deep], w1[...], preferred_element_type=F32)
        acc = acc + jnp.dot(x_ref[:, 2 * deep : 3 * deep], w2[...], preferred_element_type=F32)
        part = lax.broadcasted_iota(jnp.int32, (parts, deep), 0)
        place = lax.broadcasted_iota(jnp.int32, (parts, deep), 1)
        lasts = []
        for k in range(2):
            pick = jnp.where(place == 8 * part + (2 * n + k) % 8, 1.0, 0.0).astype(BF)
            lasts.append(jnp.dot(pick, last_ref[...], preferred_element_type=F32).astype(BF))
        acc = acc + jnp.dot(x_ref[:, 3 * deep :], jnp.concatenate(lasts, axis=1), preferred_element_type=F32)
        col = lax.broadcasted_iota(jnp.int32, (1, block), 1) + n * block
        is_key = (col >= head_width) & (col < 2 * head_width)
        out_ref[...] = (acc * jnp.where(is_key, sharp_ref[...], 1.0)).astype(BF)

    def last_tile(n):
        j = n // 4
        return (0, jnp.where(j < eights, 40 * j + 39, 117 + j))

    return pl.pallas_call(
        body,
        grid=(pairs,),
        out_shape=jax.ShapeDtypeStruct((rows, pairs * block), BF),
        in_specs=[
            VMEM,
            pl.BlockSpec((deep, block), lambda n: (0, n)),
            pl.BlockSpec((deep, block), lambda n: (0, n + 20)),
            pl.BlockSpec((deep, block), lambda n: (0, n + 40)),
            pl.BlockSpec((deep, 128), last_tile),
            VMEM,
        ],
        out_specs=pl.BlockSpec((rows, block), lambda n: (0, n)),
        compiler_params=pltpu.CompilerParams(vmem_limit_bytes=32 << 20),
        name="project",
    )(normed, packed, packed, packed, packed, sharp)


def attend(before, here, after, own_ids, key_ids):
    rows = here.shape[0]
    scale = 1.0 / math.sqrt(HD)

    def body(q_ref, kb, kh, ka, vb, vh, va, own_ref, key_ref, out_ref, bias):
        @pl.when(pl.program_id(0) == 0)
        def _():
            bias[...] = jnp.where(own_ref[...] == key_ref[...], 0.0, -1e30)

        q = q_ref[...]
        parts = [
            lax.dot_general(q, k[...], (((1,), (1,)), ((), ())), preferred_element_type=F32)
            for k in (kb, kh, ka)
        ]
        logits = jnp.concatenate(parts, axis=1) * scale + bias[...]
        peak = jnp.max(logits, axis=1, keepdims=True)
        weights = jnp.exp(logits - peak)
        total = jnp.sum(weights, axis=1, keepdims=True)
        probs = weights.astype(BF)
        value = jnp.concatenate([vb[...], vh[...], va[...]], axis=0)
        out = jnp.dot(probs, value, preferred_element_type=F32)
        out_ref[...] = (out / total).astype(BF)

    q_spec = pl.BlockSpec((rows, HD), lambda h: (0, h))
    k_here = pl.BlockSpec((rows, HD), lambda h: (0, h + HEADS))
    v_here = pl.BlockSpec((rows, HD), lambda h: (0, h + 2 * HEADS))
    k_near = pl.BlockSpec((rows, HD), lambda h: (0, h))
    v_near = pl.BlockSpec((rows, HD), lambda h: (0, h + HEADS))
    return pl.pallas_call(
        body,
        grid=(HEADS,),
        out_shape=jax.ShapeDtypeStruct((rows, HW), BF),
        in_specs=[q_spec, k_near, k_here, k_near, v_near, v_here, v_near, VMEM, VMEM],
        out_specs=q_spec,
        scratch_shapes=[pltpu.VMEM((rows, 3 * rows), F32)],
        name="attend",
    )(here, before, here, after, before, here, after, own_ids, key_ids)


def shards(
    canvas,
    conv_weight,
    conv_bias,
    score_weight,
    tile_tokens,
    tile_cell,
    tile_count,
    holder_order,
    tile_image,
    ln_gain,
    qkv_weight,
):
    axes = ("grp", "dev")
    holders = lax.axis_size("dev")
    parts = holders * lax.axis_size("grp")
    own = lax.axis_index("dev")
    counts, order = tile_count[0], holder_order[0]
    tile_len = tile_tokens.shape[1]
    held_rows = MT * tile_len

    sent = send_order(counts, order, own.reshape(1), tile_tokens)
    recv = lax.all_to_all(sent, "dev", split_axis=0, concat_axis=0, tiled=True)

    packed = lax.all_gather(pack_rows(qkv_weight), axes, axis=0, tiled=True)

    up, down = ring_pairs("grp")
    top = lax.ppermute(canvas[-1:], "grp", up)
    bottom = lax.ppermute(canvas[:1], "grp", down)
    up, down = ring_pairs("dev")

    def edge(col):
        return jnp.concatenate([top[:, col], canvas[:, col], bottom[:, col]], axis=0)

    left = lax.ppermute(edge(-1), "dev", up)
    right = lax.ppermute(edge(0), "dev", down)
    score_map = conv_scores(canvas, top, bottom, left, right, conv_weight, conv_bias, score_weight)

    ranks = jnp.arange(holders, dtype=jnp.int32)
    first = jnp.sum(jnp.where(ranks < own, counts, 0))
    place_of = jnp.sum(jnp.where(order[None, :] == ranks[:, None], ranks[None, :], 0), axis=1)
    slot_for = (place_of - first) & (holders - 1)
    cells = jnp.take(tile_cell[0], slot_for)
    send_score = jnp.take(score_map.reshape(-1), cells).astype(BF)
    recv, send_score = lax.optimization_barrier((recv, send_score))
    recv_score = lax.all_to_all(
        send_score.reshape(holders, 1, 1), "dev", split_axis=0, concat_axis=0, tiled=True
    ).reshape(holders)

    place = jnp.sum(jnp.where(order == own, ranks, 0))
    wanted = jnp.arange(MT, dtype=jnp.int32) * holders + place
    ends = jnp.sum(jnp.where(ranks[None, :] <= ranks[:, None], counts[None, :], 0), axis=1)
    source = jnp.sum((ends[None, :] <= wanted[:, None]).astype(jnp.int32), axis=1)
    held_score = jnp.take(recv_score, source).astype(F32)
    sharp = jnp.repeat(0.5 + jax.nn.softplus(held_score), tile_len)[:, None]

    normed = hold_and_norm(source, recv, ln_gain, parts)
    here = project(normed, packed, sharp, HW)
    near = here[:, HW : 3 * HW]
    before = lax.ppermute(near, "dev", up)
    after = lax.ppermute(near, "dev", down)

    all_ids = tile_image[0]
    places = own * MT - MT + jnp.arange(3 * MT, dtype=jnp.int32)
    inside = (places >= 0) & (places < all_ids.shape[0])
    near_ids = jnp.where(inside, jnp.take(all_ids, jnp.clip(places, 0, all_ids.shape[0] - 1)), -1)
    key_ids = jnp.repeat(near_ids, tile_len)
    own_ids = key_ids[held_rows : 2 * held_rows]
    attended = attend(before, here, after, own_ids[:, None], key_ids[None, :])
    return (score_map, attended)


def solution(mesh):
    placed = (
        P("grp", "dev", None),
        P(),
        P(),
        P(),
        P(("grp", "dev"), None, None),
        P("grp", "dev"),
        P("grp", None),
        P("grp", None),
        P("grp", None),
        P(),
        P(("grp", "dev"), None),
    )
    return jax.shard_map(
        shards,
        mesh=mesh,
        in_specs=placed,
        out_specs=(P("grp", "dev"), P(("grp", "dev"), None)),
        check_vma=False,
    )
```

```python
import math

import jax
import jax.numpy as jnp
import numpy as np
from jax import lax
from jax.experimental import pallas as pl
from jax.experimental.pallas import tpu as pltpu
from jax.sharding import PartitionSpec as P


HD = 128
HEADS = 13
HW = HEADS * HD
MT = 8
BF = jnp.bfloat16
F32 = jnp.float32
ANY = pl.BlockSpec(memory_space=pl.ANY)
SMEM = pl.BlockSpec(memory_space=pltpu.SMEM)
VMEM = pl.BlockSpec(memory_space=pltpu.VMEM)


def ring_pairs(axis):
    size = lax.axis_size(axis)
    up = [(i, i + 1) for i in range(size - 1)]
    return up, [(j, i) for i, j in up]


def send_order(counts, order, own, tokens):
    holders = order.shape[0]

    def body(counts_ref, order_ref, own_ref, tok_ref, out_ref, tiles, in_sems, out_sems):
        fetch = [pltpu.make_async_copy(tok_ref.at[s], tiles.at[s], in_sems.at[s]) for s in range(holders)]
        for c in fetch:
            c.start()
        first = lax.fori_loop(0, own_ref[0], lambda j, acc: acc + counts_ref[j], jnp.int32(0))

        def copy(s):
            holder = order_ref[(first + s) & (holders - 1)]
            return pltpu.make_async_copy(tiles.at[s], out_ref.at[holder], out_sems.at[s])

        for s in range(holders):
            fetch[s].wait()
            copy(s).start()
        for s in range(holders):
            copy(s).wait()

    return pl.pallas_call(
        body,
        out_shape=jax.ShapeDtypeStruct(tokens.shape, tokens.dtype),
        in_specs=[SMEM, SMEM, SMEM, ANY],
        out_specs=ANY,
        scratch_shapes=[
            pltpu.VMEM(tokens.shape, tokens.dtype),
            pltpu.SemaphoreType.DMA((holders,)),
            pltpu.SemaphoreType.DMA((holders,)),
        ],
        name="send_order",
    )(counts, order, own, tokens)


def spread_index(parts, rows):
    part, row = np.arange(parts)[:, None], np.arange(8)[None, :]
    main = [(rows * part + 8 * b + row).reshape(-1) for b in range(rows // 8)]
    return np.concatenate(main + [rows * np.arange(parts) + rows - 1]).astype(np.int32)


def hold_and_norm(source, recv, gain, parts):
    tile_len, width = recv.shape[1], recv.shape[2]
    rows = MT * tile_len
    index = spread_index(parts, width // parts)
    blocks = width // 128
    table = jnp.asarray(index.reshape(blocks, 128))

    def body(src_ref, recv_ref, gain_ref, table_ref, out_ref, tiles, normed, sems):
        copies = [
            pltpu.make_async_copy(recv_ref.at[src_ref[m]], tiles.at[m], sems.at[m]) for m in range(MT)
        ]
        for c in copies:
            c.start()
        for m in range(MT):
            copies[m].wait()
            values = tiles[m].astype(F32)
            center = jnp.mean(values, axis=1, keepdims=True)
            values = values - center
            spread = jnp.mean(values * values, axis=1, keepdims=True)
            scaled = values * lax.rsqrt(spread + 1e-06) * gain_ref[...]
            normed[m * tile_len : (m + 1) * tile_len, :] = scaled.astype(BF)
        for n in range(blocks):
            part = index[n * 128 : (n + 1) * 128]
            low = int(part.min()) // 128 * 128
            high = int(part.max()) // 128 * 128 + 128
            place = lax.broadcasted_iota(jnp.int32, (high - low, 128), 0) + low
            pick = jnp.where(place == table_ref[n : n + 1, :], 1.0, 0.0).astype(BF)
            out_ref[:, n * 128 : (n + 1) * 128] = jnp.dot(
                normed[:, low:high], pick, preferred_element_type=F32
            ).astype(BF)

    return pl.pallas_call(
        body,
        out_shape=jax.ShapeDtypeStruct((rows, width), BF),
        in_specs=[SMEM, ANY, VMEM, VMEM],
        out_specs=VMEM,
        scratch_shapes=[
            pltpu.VMEM((MT, tile_len, width), BF),
            pltpu.VMEM((rows, width), BF),
            pltpu.SemaphoreType.DMA((MT,)),
        ],
        name="hold_and_norm",
    )(source, recv, gain.reshape(1, width), table)


def conv_scores(canvas, top, bottom, left, right, weight, bias, readout):
    height, breadth, channels = canvas.shape
    hidden = weight.shape[1]
    step = 8
    pixels = step * breadth

    def side(edge):
        return jnp.concatenate([edge[0:height], edge[1 : height + 1], edge[2 : height + 2]], axis=1)

    def body(canvas_ref, top_ref, bottom_ref, left_ref, right_ref, w_ref, bias_ref, read_ref, out_ref,
             padded, lside, rside, sem):
        i = pl.program_id(0)

        def w_of(col):
            return jnp.concatenate(
                [w_ref[(row * 3 + col) * channels : (row * 3 + col + 1) * channels, :] for row in range(3)],
                axis=0,
            )

        @pl.when(i == 0)
        def _():
            fetch = pltpu.make_async_copy(canvas_ref, padded.at[pl.ds(1, height)], sem)
            fetch.start()
            padded[0:1] = top_ref[...]
            padded[height + 1 : height + 2] = bottom_ref[...]
            sides = (height // step, step, hidden)
            lside[...] = jnp.dot(left_ref[...], w_of(0), preferred_element_type=F32).reshape(sides)
            rside[...] = jnp.dot(right_ref[...], w_of(2), preferred_element_type=F32).reshape(sides)
            fetch.wait()

        window = jnp.concatenate(
            [padded[pl.ds(i * step + row, step)].reshape(pixels, channels) for row in range(3)], axis=1
        )
        before = jnp.dot(window, w_of(0), preferred_element_type=F32)
        at = jnp.dot(window, w_of(1), preferred_element_type=F32)
        after = jnp.dot(window, w_of(2), preferred_element_type=F32)
        before = pltpu.roll(before, 1, 0).reshape(step, breadth, hidden)
        after = pltpu.roll(after, pixels - 1, 0).reshape(step, breadth, hidden)
        col = lax.broadcasted_iota(jnp.int32, (step, breadth, hidden), 1)
        lrow = lside[i]
        rrow = rside[i]
        before = jnp.where(col == 0, lrow[:, None, :], before)
        after = jnp.where(col == breadth - 1, rrow[:, None, :], after)
        x = (before + after).reshape(pixels, hidden) + at + bias_ref[...]
        inner = math.sqrt(2.0 / math.pi) * (x + 0.044715 * (x * x * x))
        h = x * (0.5 * (1.0 + jnp.tanh(inner)))
        h = h * read_ref[...]
        half = h[:, 0:128]
        for k in range(1, hidden // 128):
            half = half + h[:, k * 128 : (k + 1) * 128]
        ones = jnp.ones((8, 128), F32)
        score = lax.dot_general(
            ones, half, (((1,), (1,)), ((), ())), precision=lax.Precision.HIGHEST, preferred_element_type=F32
        )
        for r in range(step):
            out_ref[0, r : r + 1, :] = score[0:1, r * breadth : (r + 1) * breadth]

    out = pl.pallas_call(
        body,
        grid=(height // step,),
        out_shape=jax.ShapeDtypeStruct((height // step, step, breadth), F32),
        in_specs=[ANY] + [pl.BlockSpec(memory_space=pltpu.VMEM)] * 7,
        out_specs=pl.BlockSpec((1, step, breadth), lambda i: (i, 0, 0)),
        scratch_shapes=[
            pltpu.VMEM((height + 2, breadth, channels), BF),
            pltpu.VMEM((height // step, step, hidden), F32),
            pltpu.VMEM((height // step, step, hidden), F32),
            pltpu.SemaphoreType.DMA,
        ],
        compiler_params=pltpu.CompilerParams(vmem_limit_bytes=32 << 20),
        name="conv_scores",
    )(canvas, top, bottom, side(left), side(right), weight, bias.reshape(1, hidden), readout.reshape(1, hidden))
    return out.reshape(height, breadth)


def pack_rows(weight):
    rows, cols = weight.shape
    eights, tiles = rows // 8, cols // 128
    spare = -(-tiles // 8)

    def body(w_ref, out_ref):
        w = w_ref[...].astype(F32)
        zero = jnp.zeros((1, 128), F32)
        for j in range(spare):
            pieces = [
                w[rows - 1 : rows, t * 128 : (t + 1) * 128] if t < tiles else zero
                for t in range(8 * j, 8 * j + 8)
            ]
            out_ref[:, j * 128 : (j + 1) * 128] = jnp.concatenate(pieces, axis=0).astype(BF)
        for b in range(eights):
            at = spare * 128 + b * cols
            out_ref[:, at : at + cols] = w[8 * b : 8 * b + 8].astype(BF)

    return pl.pallas_call(
        body,
        out_shape=jax.ShapeDtypeStruct((8, spare * 128 + eights * cols), BF),
        in_specs=[VMEM],
        out_specs=VMEM,
        name="pack_rows",
    )(weight)


def project_and_attend(before, here, after, packed, sharp, own_ids, key_ids):
    rows, width = here.shape
    deep = packed.shape[0]
    eights, parts = width // deep, deep // 8
    near = 3 * rows
    spare = -(-3 * HEADS // 8)
    scale = 1.0 / math.sqrt(HD)

    def body(xb, xh, xa, ext, *refs):
        w_refs = refs[:9]
        sharp_ref, own_ref, key_ref, out_ref, x, bias, wide, lasts, q_buf, k_buf, v_buf = refs[9:]
        n = pl.program_id(0)
        head = jnp.minimum(n, HEADS - 1)

        @pl.when(n == 0)
        def _():
            x[0:rows] = xb[...]
            x[rows : 2 * rows] = xh[...]
            x[2 * rows :] = xa[...]
            bias[...] = jnp.where(own_ref[...] == key_ref[...], 0.0, -1e30)
            for j in range(spare):
                wide[j] = ext[:, j * 128 : (j + 1) * 128].astype(F32)
            for j in range(spare):
                for s in range(8):
                    lasts[8 * j + s] = wide[j, pl.ds(s, parts, stride=8), :].astype(BF)
            q_buf[1] = jnp.zeros((rows, HD), BF)
            k_buf[1] = jnp.zeros((near, HD), BF)
            v_buf[1] = jnp.zeros((near, HD), BF)

        done = (n + 1) % 2
        logits = lax.dot_general(
            q_buf[done], k_buf[done], (((1,), (1,)), ((), ())), preferred_element_type=F32
        )
        logits = logits * scale + bias[...]
        peak = jnp.max(logits, axis=1, keepdims=True)
        weights = jnp.exp(logits - peak)
        total = jnp.sum(weights, axis=1, keepdims=True)
        result = jnp.dot(weights.astype(BF), v_buf[done], preferred_element_type=F32)
        out_ref[...] = (result / total).astype(BF)

        q = jnp.zeros((rows, HD), F32)
        kv = jnp.zeros((near, 2 * HD), F32)
        for b in range(eights):
            at = b * deep
            q = q + jnp.dot(xh[:, at : at + deep], w_refs[b][...], preferred_element_type=F32)
            both = jnp.concatenate([w_refs[3 + b][...], w_refs[6 + b][...]], axis=1)
            kv = kv + jnp.dot(x[:, at : at + deep], both, preferred_element_type=F32)
        at = eights * deep
        q = q + jnp.dot(xh[:, at:], lasts[head], preferred_element_type=F32)
        both = jnp.concatenate([lasts[head + HEADS], lasts[head + 2 * HEADS]], axis=1)
        kv = kv + jnp.dot(x[:, at:], both, preferred_element_type=F32)
        new = n % 2
        q_buf[new] = q.astype(BF)
        k_buf[new] = (kv[:, :HD] * sharp_ref[...]).astype(BF)
        v_buf[new] = kv[:, HD:].astype(BF)

    def w_spec(b, kind):
        first = spare + b * 3 * HEADS + kind * HEADS
        return pl.BlockSpec((deep, HD), lambda n: (0, first + jnp.minimum(n, HEADS - 1)))

    return pl.pallas_call(
        body,
        grid=(HEADS + 1,),
        out_shape=jax.ShapeDtypeStruct((rows, HW), BF),
        in_specs=[VMEM, VMEM, VMEM, pl.BlockSpec((deep, spare * 128), lambda n: (0, 0))]
        + [w_spec(b, kind) for kind in range(3) for b in range(3)]
        + [VMEM, VMEM, VMEM],
        out_specs=pl.BlockSpec((rows, HD), lambda n: (0, jnp.maximum(n - 1, 0))),
        scratch_shapes=[
            pltpu.VMEM((near, width), BF),
            pltpu.VMEM((rows, near), F32),
            pltpu.VMEM((spare, deep, 128), F32),
            pltpu.VMEM((8 * spare, parts, HD), BF),
            pltpu.VMEM((2, rows, HD), BF),
            pltpu.VMEM((2, near, HD), BF),
            pltpu.VMEM((2, near, HD), BF),
        ],
        compiler_params=pltpu.CompilerParams(vmem_limit_bytes=48 << 20),
        name="project_and_attend",
    )(before, here, after, *([packed] * 10), sharp, own_ids, key_ids)


def shards(
    canvas,
    conv_weight,
    conv_bias,
    score_weight,
    tile_tokens,
    tile_cell,
    tile_count,
    holder_order,
    tile_image,
    ln_gain,
    qkv_weight,
):
    axes = ("grp", "dev")
    holders = lax.axis_size("dev")
    parts = holders * lax.axis_size("grp")
    own = lax.axis_index("dev")
    counts, order = tile_count[0], holder_order[0]
    tile_len = tile_tokens.shape[1]
    held_rows = MT * tile_len

    sent = send_order(counts, order, own.reshape(1), tile_tokens)
    recv = lax.all_to_all(sent, "dev", split_axis=0, concat_axis=0, tiled=True)

    packed = lax.all_gather(pack_rows(qkv_weight), axes, axis=0, tiled=True)

    up, down = ring_pairs("grp")
    top = lax.ppermute(canvas[-1:], "grp", up)
    bottom = lax.ppermute(canvas[:1], "grp", down)
    up, down = ring_pairs("dev")

    def edge(col):
        return jnp.concatenate([top[:, col], canvas[:, col], bottom[:, col]], axis=0)

    left = lax.ppermute(edge(-1), "dev", up)
    right = lax.ppermute(edge(0), "dev", down)
    score_map = conv_scores(canvas, top, bottom, left, right, conv_weight, conv_bias, score_weight)

    ranks = jnp.arange(holders, dtype=jnp.int32)
    first = jnp.sum(jnp.where(ranks < own, counts, 0))
    place_of = jnp.sum(jnp.where(order[None, :] == ranks[:, None], ranks[None, :], 0), axis=1)
    slot_for = (place_of - first) & (holders - 1)
    cells = jnp.take(tile_cell[0], slot_for)
    send_score = jnp.take(score_map.reshape(-1), cells).astype(BF)
    recv, send_score = lax.optimization_barrier((recv, send_score))
    recv_score = lax.all_to_all(
        send_score.reshape(holders, 1, 1), "dev", split_axis=0, concat_axis=0, tiled=True
    ).reshape(holders)

    place = jnp.sum(jnp.where(order == own, ranks, 0))
    wanted = jnp.arange(MT, dtype=jnp.int32) * holders + place
    ends = jnp.sum(jnp.where(ranks[None, :] <= ranks[:, None], counts[None, :], 0), axis=1)
    source = jnp.sum((ends[None, :] <= wanted[:, None]).astype(jnp.int32), axis=1)
    held_score = jnp.take(recv_score, source).reshape(1, MT)
    near_score = jnp.concatenate(
        [lax.ppermute(held_score, "dev", up), held_score, lax.ppermute(held_score, "dev", down)], axis=1
    )
    sharp = jnp.repeat(0.5 + jax.nn.softplus(near_score[0].astype(F32)), tile_len)[:, None]

    here = hold_and_norm(source, recv, ln_gain, parts)
    before = lax.ppermute(here, "dev", up)
    after = lax.ppermute(here, "dev", down)

    all_ids = tile_image[0]
    places = own * MT - MT + jnp.arange(3 * MT, dtype=jnp.int32)
    inside = (places >= 0) & (places < all_ids.shape[0])
    near_ids = jnp.where(inside, jnp.take(all_ids, jnp.clip(places, 0, all_ids.shape[0] - 1)), -1)
    key_ids = jnp.repeat(near_ids, tile_len)
    own_ids = key_ids[held_rows : 2 * held_rows]
    attended = project_and_attend(before, here, after, packed, sharp, own_ids[:, None], key_ids[None, :])
    return (score_map, attended)


def solution(mesh):
    placed = (
        P("grp", "dev", None),
        P(),
        P(),
        P(),
        P(("grp", "dev"), None, None),
        P("grp", "dev"),
        P("grp", None),
        P("grp", None),
        P("grp", None),
        P(),
        P(("grp", "dev"), None),
    )
    return jax.shard_map(
        shards,
        mesh=mesh,
        in_specs=placed,
        out_specs=(P("grp", "dev"), P(("grp", "dev"), None)),
        check_vma=False,
    )
```

```python
import math

import jax
import jax.numpy as jnp
import numpy as np
from jax import lax
from jax.experimental import pallas as pl
from jax.experimental.pallas import tpu as pltpu
from jax.sharding import PartitionSpec as P


HD = 128
HEADS = 13
HW = HEADS * HD
MT = 8
BF = jnp.bfloat16
F32 = jnp.float32
ANY = pl.BlockSpec(memory_space=pl.ANY)
SMEM = pl.BlockSpec(memory_space=pltpu.SMEM)
VMEM = pl.BlockSpec(memory_space=pltpu.VMEM)


def ring_pairs(axis):
    size = lax.axis_size(axis)
    up = [(i, i + 1) for i in range(size - 1)]
    return up, [(j, i) for i, j in up]


def send_order(counts, order, own, tokens):
    holders = order.shape[0]

    def body(counts_ref, order_ref, own_ref, tok_ref, out_ref, tiles, in_sems, out_sems):
        fetch = [pltpu.make_async_copy(tok_ref.at[s], tiles.at[s], in_sems.at[s]) for s in range(holders)]
        for c in fetch:
            c.start()
        first = lax.fori_loop(0, own_ref[0], lambda j, acc: acc + counts_ref[j], jnp.int32(0))

        def copy(s):
            holder = order_ref[(first + s) & (holders - 1)]
            return pltpu.make_async_copy(tiles.at[s], out_ref.at[holder], out_sems.at[s])

        for s in range(holders):
            fetch[s].wait()
            copy(s).start()
        for s in range(holders):
            copy(s).wait()

    return pl.pallas_call(
        body,
        out_shape=jax.ShapeDtypeStruct(tokens.shape, tokens.dtype),
        in_specs=[SMEM, SMEM, SMEM, ANY],
        out_specs=ANY,
        scratch_shapes=[
            pltpu.VMEM(tokens.shape, tokens.dtype),
            pltpu.SemaphoreType.DMA((holders,)),
            pltpu.SemaphoreType.DMA((holders,)),
        ],
        name="send_order",
    )(counts, order, own, tokens)


def spread_index(parts, rows):
    part, row = np.arange(parts)[:, None], np.arange(8)[None, :]
    main = [(rows * part + 8 * b + row).reshape(-1) for b in range(rows // 8)]
    return np.concatenate(main + [rows * np.arange(parts) + rows - 1]).astype(np.int32)


def hold_and_norm(source, recv, gain, parts):
    tile_len, width = recv.shape[1], recv.shape[2]
    rows = MT * tile_len
    index = spread_index(parts, width // parts)
    blocks = width // 128
    table = jnp.asarray(index.reshape(blocks, 128))

    def body(src_ref, recv_ref, gain_ref, table_ref, out_ref, tiles, normed, sems):
        copies = [
            pltpu.make_async_copy(recv_ref.at[src_ref[m]], tiles.at[m], sems.at[m]) for m in range(MT)
        ]
        for c in copies:
            c.start()
        for m in range(MT):
            copies[m].wait()
            values = tiles[m].astype(F32)
            center = jnp.mean(values, axis=1, keepdims=True)
            values = values - center
            spread = jnp.mean(values * values, axis=1, keepdims=True)
            scaled = values * lax.rsqrt(spread + 1e-06) * gain_ref[...]
            normed[m * tile_len : (m + 1) * tile_len, :] = scaled.astype(BF)
        for n in range(blocks):
            part = index[n * 128 : (n + 1) * 128]
            low = int(part.min()) // 128 * 128
            high = int(part.max()) // 128 * 128 + 128
            place = lax.broadcasted_iota(jnp.int32, (high - low, 128), 0) + low
            pick = jnp.where(place == table_ref[n : n + 1, :], 1.0, 0.0).astype(BF)
            out_ref[:, n * 128 : (n + 1) * 128] = jnp.dot(
                normed[:, low:high], pick, preferred_element_type=F32
            ).astype(BF)

    return pl.pallas_call(
        body,
        out_shape=jax.ShapeDtypeStruct((rows, width), BF),
        in_specs=[SMEM, ANY, VMEM, VMEM],
        out_specs=VMEM,
        scratch_shapes=[
            pltpu.VMEM((MT, tile_len, width), BF),
            pltpu.VMEM((rows, width), BF),
            pltpu.SemaphoreType.DMA((MT,)),
        ],
        name="hold_and_norm",
    )(source, recv, gain.reshape(1, width), table)


def conv_scores(canvas, top, bottom, left, right, weight, bias, readout):
    height, breadth, channels = canvas.shape
    hidden = weight.shape[1]
    step = 8
    pixels = step * breadth

    def side(edge):
        return jnp.concatenate([edge[0:height], edge[1 : height + 1], edge[2 : height + 2]], axis=1)

    def body(canvas_ref, top_ref, bottom_ref, left_ref, right_ref, w_ref, bias_ref, read_ref, out_ref,
             padded, lside, rside, sem):
        i = pl.program_id(0)

        def w_of(col):
            return jnp.concatenate(
                [w_ref[(row * 3 + col) * channels : (row * 3 + col + 1) * channels, :] for row in range(3)],
                axis=0,
            )

        @pl.when(i == 0)
        def _():
            fetch = pltpu.make_async_copy(canvas_ref, padded.at[pl.ds(1, height)], sem)
            fetch.start()
            padded[0:1] = top_ref[...]
            padded[height + 1 : height + 2] = bottom_ref[...]
            sides = (height // step, step, hidden)
            lside[...] = jnp.dot(left_ref[...], w_of(0), preferred_element_type=F32).reshape(sides)
            rside[...] = jnp.dot(right_ref[...], w_of(2), preferred_element_type=F32).reshape(sides)
            fetch.wait()

        window = jnp.concatenate(
            [padded[pl.ds(i * step + row, step)].reshape(pixels, channels) for row in range(3)], axis=1
        )
        before = jnp.dot(window, w_of(0), preferred_element_type=F32)
        at = jnp.dot(window, w_of(1), preferred_element_type=F32)
        after = jnp.dot(window, w_of(2), preferred_element_type=F32)
        before = pltpu.roll(before, 1, 0).reshape(step, breadth, hidden)
        after = pltpu.roll(after, pixels - 1, 0).reshape(step, breadth, hidden)
        col = lax.broadcasted_iota(jnp.int32, (step, breadth, hidden), 1)
        lrow = lside[i]
        rrow = rside[i]
        before = jnp.where(col == 0, lrow[:, None, :], before)
        after = jnp.where(col == breadth - 1, rrow[:, None, :], after)
        x = (before + after).reshape(pixels, hidden) + at + bias_ref[...]
        inner = math.sqrt(2.0 / math.pi) * (x + 0.044715 * (x * x * x))
        h = x * (0.5 * (1.0 + jnp.tanh(inner)))
        h = h * read_ref[...]
        half = h[:, 0:128]
        for k in range(1, hidden // 128):
            half = half + h[:, k * 128 : (k + 1) * 128]
        ones = jnp.ones((8, 128), F32)
        score = lax.dot_general(
            ones, half, (((1,), (1,)), ((), ())), precision=lax.Precision.HIGHEST, preferred_element_type=F32
        )
        for r in range(step):
            out_ref[0, r : r + 1, :] = score[0:1, r * breadth : (r + 1) * breadth]

    out = pl.pallas_call(
        body,
        grid=(height // step,),
        out_shape=jax.ShapeDtypeStruct((height // step, step, breadth), F32),
        in_specs=[ANY] + [pl.BlockSpec(memory_space=pltpu.VMEM)] * 7,
        out_specs=pl.BlockSpec((1, step, breadth), lambda i: (i, 0, 0)),
        scratch_shapes=[
            pltpu.VMEM((height + 2, breadth, channels), BF),
            pltpu.VMEM((height // step, step, hidden), F32),
            pltpu.VMEM((height // step, step, hidden), F32),
            pltpu.SemaphoreType.DMA,
        ],
        compiler_params=pltpu.CompilerParams(vmem_limit_bytes=32 << 20),
        name="conv_scores",
    )(canvas, top, bottom, side(left), side(right), weight, bias.reshape(1, hidden), readout.reshape(1, hidden))
    return out.reshape(height, breadth)


def pack_rows(weight):
    rows, cols = weight.shape
    eights, tiles = rows // 8, cols // 128
    spare = -(-tiles // 8)

    def body(w_ref, out_ref):
        w = w_ref[...].astype(F32)
        zero = jnp.zeros((1, 128), F32)
        for j in range(spare):
            pieces = [
                w[rows - 1 : rows, t * 128 : (t + 1) * 128] if t < tiles else zero
                for t in range(8 * j, 8 * j + 8)
            ]
            out_ref[:, j * 128 : (j + 1) * 128] = jnp.concatenate(pieces, axis=0).astype(BF)
        for b in range(eights):
            at = spare * 128 + b * cols
            out_ref[:, at : at + cols] = w[8 * b : 8 * b + 8].astype(BF)

    return pl.pallas_call(
        body,
        out_shape=jax.ShapeDtypeStruct((8, spare * 128 + eights * cols), BF),
        in_specs=[VMEM],
        out_specs=VMEM,
        name="pack_rows",
    )(weight)


def project_and_attend(before, here, after, packed, sharp, own_ids, key_ids):
    rows, width = here.shape
    deep = packed.shape[0]
    eights, parts = width // deep, deep // 8
    near = 3 * rows
    spare = -(-3 * HEADS // 8)
    scale = 1.0 / math.sqrt(HD)

    def body(xb, xh, xa, ext, *refs):
        w_refs = refs[:9]
        sharp_ref, own_ref, key_ref, out_ref, x, bias, wide, lasts, q_buf, k_buf, v_buf = refs[9:]
        n = pl.program_id(0)
        head = jnp.minimum(n, HEADS - 1)

        @pl.when(n == 0)
        def _():
            x[0:rows] = xb[...]
            x[rows : 2 * rows] = xh[...]
            x[2 * rows :] = xa[...]
            bias[...] = jnp.where(own_ref[...] == key_ref[...], 0.0, -1e30)
            for j in range(spare):
                wide[j] = ext[:, j * 128 : (j + 1) * 128].astype(F32)
            for j in range(spare):
                for s in range(8):
                    lasts[8 * j + s] = wide[j, pl.ds(s, parts, stride=8), :].astype(BF)
            q_buf[1] = jnp.zeros((rows, HD), BF)
            k_buf[1] = jnp.zeros((near, HD), BF)
            v_buf[1] = jnp.zeros((near, HD), BF)

        done = (n + 1) % 2
        logits = lax.dot_general(
            q_buf[done], k_buf[done], (((1,), (1,)), ((), ())), preferred_element_type=F32
        )
        logits = logits * scale + bias[...]
        peak = jnp.max(logits, axis=1, keepdims=True)
        weights = jnp.exp(logits - peak)
        total = jnp.sum(weights, axis=1, keepdims=True)
        result = jnp.dot(weights.astype(BF), v_buf[done], preferred_element_type=F32)
        out_ref[...] = (result / total).astype(BF)

        q = jnp.zeros((rows, HD), F32)
        kv = jnp.zeros((near, 2 * HD), F32)
        for b in range(eights):
            at = b * deep
            q = q + jnp.dot(xh[:, at : at + deep], w_refs[b][...], preferred_element_type=F32)
            both = jnp.concatenate([w_refs[3 + b][...], w_refs[6 + b][...]], axis=1)
            kv = kv + jnp.dot(x[:, at : at + deep], both, preferred_element_type=F32)
        at = eights * deep
        q = q + jnp.dot(xh[:, at:], lasts[head], preferred_element_type=F32)
        both = jnp.concatenate([lasts[head + HEADS], lasts[head + 2 * HEADS]], axis=1)
        kv = kv + jnp.dot(x[:, at:], both, preferred_element_type=F32)
        new = n % 2
        q_buf[new] = q.astype(BF)
        k_buf[new] = (kv[:, :HD] * sharp_ref[...]).astype(BF)
        v_buf[new] = kv[:, HD:].astype(BF)

    def w_spec(b, kind):
        first = spare + b * 3 * HEADS + kind * HEADS
        return pl.BlockSpec((deep, HD), lambda n: (0, first + jnp.minimum(n, HEADS - 1)))

    return pl.pallas_call(
        body,
        grid=(HEADS + 1,),
        out_shape=jax.ShapeDtypeStruct((rows, HW), BF),
        in_specs=[VMEM, VMEM, VMEM, pl.BlockSpec((deep, spare * 128), lambda n: (0, 0))]
        + [w_spec(b, kind) for kind in range(3) for b in range(3)]
        + [VMEM, VMEM, VMEM],
        out_specs=pl.BlockSpec((rows, HD), lambda n: (0, jnp.maximum(n - 1, 0))),
        scratch_shapes=[
            pltpu.VMEM((near, width), BF),
            pltpu.VMEM((rows, near), F32),
            pltpu.VMEM((spare, deep, 128), F32),
            pltpu.VMEM((8 * spare, parts, HD), BF),
            pltpu.VMEM((2, rows, HD), BF),
            pltpu.VMEM((2, near, HD), BF),
            pltpu.VMEM((2, near, HD), BF),
        ],
        compiler_params=pltpu.CompilerParams(vmem_limit_bytes=48 << 20),
        name="project_and_attend",
    )(before, here, after, *([packed] * 10), sharp, own_ids, key_ids)


def shards(
    canvas,
    conv_weight,
    conv_bias,
    score_weight,
    tile_tokens,
    tile_cell,
    tile_count,
    holder_order,
    tile_image,
    ln_gain,
    qkv_weight,
):
    axes = ("grp", "dev")
    holders = lax.axis_size("dev")
    parts = holders * lax.axis_size("grp")
    own = lax.axis_index("dev")
    counts, order = tile_count[0], holder_order[0]
    tile_len = tile_tokens.shape[1]
    held_rows = MT * tile_len

    sent = send_order(counts, order, own.reshape(1), tile_tokens)
    recv = lax.all_to_all(sent, "dev", split_axis=0, concat_axis=0, tiled=True)

    packed = lax.all_gather(pack_rows(qkv_weight), axes, axis=0, tiled=True)

    up, down = ring_pairs("grp")
    top = lax.ppermute(canvas[-1:], "grp", up)
    bottom = lax.ppermute(canvas[:1], "grp", down)
    up, down = ring_pairs("dev")

    def edge(col):
        return jnp.concatenate([top[:, col], canvas[:, col], bottom[:, col]], axis=0)

    left = lax.ppermute(edge(-1), "dev", up)
    right = lax.ppermute(edge(0), "dev", down)
    score_map = conv_scores(canvas, top, bottom, left, right, conv_weight, conv_bias, score_weight)

    ranks = jnp.arange(holders, dtype=jnp.int32)
    first = jnp.sum(jnp.where(ranks < own, counts, 0))
    place_of = jnp.sum(jnp.where(order[None, :] == ranks[:, None], ranks[None, :], 0), axis=1)
    slot_for = (place_of - first) & (holders - 1)
    cells = jnp.take(tile_cell[0], slot_for)
    send_score = jnp.take(score_map.reshape(-1), cells).astype(BF)
    send_score = jnp.stack([jnp.roll(send_score, 1), send_score, jnp.roll(send_score, -1)], axis=1)
    recv, send_score = lax.optimization_barrier((recv, send_score))
    recv_score = lax.all_to_all(send_score, "dev", split_axis=0, concat_axis=0, tiled=True)

    near_holders = jnp.clip(own + jnp.arange(-1, 2, dtype=jnp.int32), 0, holders - 1)
    places = jnp.sum(jnp.where(order[None, :] == near_holders[:, None], ranks[None, :], 0), axis=1)
    wanted = jnp.arange(MT, dtype=jnp.int32)[None, :] * holders + places[:, None]
    ends = jnp.sum(jnp.where(ranks[None, :] <= ranks[:, None], counts[None, :], 0), axis=1)
    source = jnp.sum((ends <= wanted[:, :, None]).astype(jnp.int32), axis=2)
    picked = source[:, :, None] == ranks
    near_score = jnp.sum(jnp.where(picked, recv_score.astype(F32).T[:, None, :], 0.0), axis=2)
    sharp = jnp.repeat(0.5 + jax.nn.softplus(near_score.reshape(-1)), tile_len)[:, None]

    here = hold_and_norm(source[1], recv, ln_gain, parts)
    before = lax.ppermute(here, "dev", up)
    after = lax.ppermute(here, "dev", down)

    all_ids = tile_image[0]
    places = own * MT - MT + jnp.arange(3 * MT, dtype=jnp.int32)
    inside = (places >= 0) & (places < all_ids.shape[0])
    near_ids = jnp.where(inside, jnp.take(all_ids, jnp.clip(places, 0, all_ids.shape[0] - 1)), -1)
    key_ids = jnp.repeat(near_ids, tile_len)
    own_ids = key_ids[held_rows : 2 * held_rows]
    attended = project_and_attend(before, here, after, packed, sharp, own_ids[:, None], key_ids[None, :])
    return (score_map, attended)


def solution(mesh):
    placed = (
        P("grp", "dev", None),
        P(),
        P(),
        P(),
        P(("grp", "dev"), None, None),
        P("grp", "dev"),
        P("grp", None),
        P("grp", None),
        P("grp", None),
        P(),
        P(("grp", "dev"), None),
    )
    return jax.shard_map(
        shards,
        mesh=mesh,
        in_specs=placed,
        out_specs=(P("grp", "dev"), P(("grp", "dev"), None)),
        check_vma=False,
    )
```

```python
import math

import jax
import jax.numpy as jnp
import numpy as np
from jax import lax
from jax.experimental import pallas as pl
from jax.experimental.pallas import tpu as pltpu
from jax.sharding import PartitionSpec as P


HD = 128
HEADS = 13
HW = HEADS * HD
MT = 8
FIRST = 11
BF = jnp.bfloat16
F32 = jnp.float32
ANY = pl.BlockSpec(memory_space=pl.ANY)
SMEM = pl.BlockSpec(memory_space=pltpu.SMEM)
VMEM = pl.BlockSpec(memory_space=pltpu.VMEM)


def ring_pairs(axis):
    size = lax.axis_size(axis)
    up = [(i, i + 1) for i in range(size - 1)]
    return up, [(j, i) for i, j in up]


def dev_shift(axis, shift):
    place = {"y": 8, "z": 2}[axis]
    pairs = []
    for d in range(lax.axis_size("dev")):
        here = d // place % 4
        pairs.append((d, d + ((here + shift) % 4 - here) * place))
    return pairs


def spread(value, axis):
    here = lax.axis_index("dev") // {"y": 8, "z": 2}[axis] % 4
    out = jnp.zeros((4,) + value.shape, value.dtype)
    out = lax.dynamic_update_index_in_dim(out, value, here, 0)
    for shift in (1, -1, 2):
        got = lax.ppermute(value, "dev", dev_shift(axis, shift))
        out = lax.dynamic_update_index_in_dim(out, got, (here - shift) % 4, 0)
    return out


def gather_rows(block):
    block = spread(block, "z")
    block = spread(block, "y")
    block = block.reshape(-1, block.shape[-1])
    grp, core = lax.axis_index("grp"), lax.axis_index("dev") % 2
    pieces = [(0, block)] + [
        (shift, lax.ppermute(block, "grp", [(i, (i + shift) % 4) for i in range(4)])) for shift in (1, -1, 2)
    ]
    cores = [(d, d ^ 1) for d in range(lax.axis_size("dev"))]
    out = jnp.zeros((4, 2) + block.shape, block.dtype)
    for shift, piece in pieces:
        other = lax.ppermute(piece, "dev", cores)
        row = (grp - shift) % 4
        out = lax.dynamic_update_slice(out, piece[None, None], (row, core, 0, 0))
        out = lax.dynamic_update_slice(out, other[None, None], (row, 1 - core, 0, 0))
    return out.reshape(-1, block.shape[-1])


def send_order(counts, order, own, tokens):
    holders = order.shape[0]

    def body(counts_ref, order_ref, own_ref, tok_ref, out_ref, tiles, in_sems, out_sems):
        fetch = [pltpu.make_async_copy(tok_ref.at[s], tiles.at[s], in_sems.at[s]) for s in range(holders)]
        for c in fetch:
            c.start()
        first = lax.fori_loop(0, own_ref[0], lambda j, acc: acc + counts_ref[j], jnp.int32(0))

        def copy(s):
            holder = order_ref[(first + s) & (holders - 1)]
            return pltpu.make_async_copy(tiles.at[s], out_ref.at[holder], out_sems.at[s])

        for s in range(holders):
            fetch[s].wait()
            copy(s).start()
        for s in range(holders):
            copy(s).wait()

    return pl.pallas_call(
        body,
        out_shape=jax.ShapeDtypeStruct(tokens.shape, tokens.dtype),
        in_specs=[SMEM, SMEM, SMEM, ANY],
        out_specs=ANY,
        scratch_shapes=[
            pltpu.VMEM(tokens.shape, tokens.dtype),
            pltpu.SemaphoreType.DMA((holders,)),
            pltpu.SemaphoreType.DMA((holders,)),
        ],
        name="send_order",
    )(counts, order, own, tokens)


def spread_index(parts, rows):
    part, row = np.arange(parts)[:, None], np.arange(8)[None, :]
    main = [(rows * part + 8 * b + row).reshape(-1) for b in range(rows // 8)]
    return np.concatenate(main + [rows * np.arange(parts) + rows - 1]).astype(np.int32)


def hold_and_norm(source, recv, gain, parts):
    tile_len, width = recv.shape[1], recv.shape[2]
    rows = MT * tile_len
    index = spread_index(parts, width // parts)
    blocks = width // 128
    table = jnp.asarray(index.reshape(blocks, 128))

    def body(src_ref, recv_ref, gain_ref, table_ref, out_ref, tiles, normed, sems):
        copies = [
            pltpu.make_async_copy(recv_ref.at[src_ref[m]], tiles.at[m], sems.at[m]) for m in range(MT)
        ]
        for c in copies:
            c.start()
        for m in range(MT):
            copies[m].wait()
            values = tiles[m].astype(F32)
            center = jnp.mean(values, axis=1, keepdims=True)
            values = values - center
            spread = jnp.mean(values * values, axis=1, keepdims=True)
            scaled = values * lax.rsqrt(spread + 1e-06) * gain_ref[...]
            normed[m * tile_len : (m + 1) * tile_len, :] = scaled.astype(BF)
        for n in range(blocks):
            part = index[n * 128 : (n + 1) * 128]
            low = int(part.min()) // 128 * 128
            high = int(part.max()) // 128 * 128 + 128
            place = lax.broadcasted_iota(jnp.int32, (high - low, 128), 0) + low
            pick = jnp.where(place == table_ref[n : n + 1, :], 1.0, 0.0).astype(BF)
            out_ref[:, n * 128 : (n + 1) * 128] = jnp.dot(
                normed[:, low:high], pick, preferred_element_type=F32
            ).astype(BF)

    return pl.pallas_call(
        body,
        out_shape=jax.ShapeDtypeStruct((rows, width), BF),
        in_specs=[SMEM, ANY, VMEM, VMEM],
        out_specs=VMEM,
        scratch_shapes=[
            pltpu.VMEM((MT, tile_len, width), BF),
            pltpu.VMEM((rows, width), BF),
            pltpu.SemaphoreType.DMA((MT,)),
        ],
        name="hold_and_norm",
    )(source, recv, gain.reshape(1, width), table)


def conv_scores(canvas, top, bottom, left, right, weight, bias, readout):
    height, breadth, channels = canvas.shape
    hidden = weight.shape[1]
    step = 8
    pixels = step * breadth

    def side(edge):
        return jnp.concatenate([edge[0:height], edge[1 : height + 1], edge[2 : height + 2]], axis=1)

    def body(canvas_ref, top_ref, bottom_ref, left_ref, right_ref, w_ref, bias_ref, read_ref, out_ref,
             padded, lside, rside, sem):
        i = pl.program_id(0)

        def w_of(col):
            return jnp.concatenate(
                [w_ref[(row * 3 + col) * channels : (row * 3 + col + 1) * channels, :] for row in range(3)],
                axis=0,
            )

        @pl.when(i == 0)
        def _():
            fetch = pltpu.make_async_copy(canvas_ref, padded.at[pl.ds(1, height)], sem)
            fetch.start()
            padded[0:1] = top_ref[...]
            padded[height + 1 : height + 2] = bottom_ref[...]
            sides = (height // step, step, hidden)
            lside[...] = jnp.dot(left_ref[...], w_of(0), preferred_element_type=F32).reshape(sides)
            rside[...] = jnp.dot(right_ref[...], w_of(2), preferred_element_type=F32).reshape(sides)
            fetch.wait()

        window = jnp.concatenate(
            [padded[pl.ds(i * step + row, step)].reshape(pixels, channels) for row in range(3)], axis=1
        )
        before = jnp.dot(window, w_of(0), preferred_element_type=F32)
        at = jnp.dot(window, w_of(1), preferred_element_type=F32)
        after = jnp.dot(window, w_of(2), preferred_element_type=F32)
        before = pltpu.roll(before, 1, 0).reshape(step, breadth, hidden)
        after = pltpu.roll(after, pixels - 1, 0).reshape(step, breadth, hidden)
        col = lax.broadcasted_iota(jnp.int32, (step, breadth, hidden), 1)
        lrow = lside[i]
        rrow = rside[i]
        before = jnp.where(col == 0, lrow[:, None, :], before)
        after = jnp.where(col == breadth - 1, rrow[:, None, :], after)
        x = (before + after).reshape(pixels, hidden) + at + bias_ref[...]
        inner = math.sqrt(2.0 / math.pi) * (x + 0.044715 * (x * x * x))
        h = x * (0.5 * (1.0 + jnp.tanh(inner)))
        h = h * read_ref[...]
        half = h[:, 0:128]
        for k in range(1, hidden // 128):
            half = half + h[:, k * 128 : (k + 1) * 128]
        ones = jnp.ones((8, 128), F32)
        score = lax.dot_general(
            ones, half, (((1,), (1,)), ((), ())), precision=lax.Precision.HIGHEST, preferred_element_type=F32
        )
        for r in range(step):
            out_ref[0, r : r + 1, :] = score[0:1, r * breadth : (r + 1) * breadth]

    out = pl.pallas_call(
        body,
        grid=(height // step,),
        out_shape=jax.ShapeDtypeStruct((height // step, step, breadth), F32),
        in_specs=[ANY] + [pl.BlockSpec(memory_space=pltpu.VMEM)] * 7,
        out_specs=pl.BlockSpec((1, step, breadth), lambda i: (i, 0, 0)),
        scratch_shapes=[
            pltpu.VMEM((height + 2, breadth, channels), BF),
            pltpu.VMEM((height // step, step, hidden), F32),
            pltpu.VMEM((height // step, step, hidden), F32),
            pltpu.SemaphoreType.DMA,
        ],
        compiler_params=pltpu.CompilerParams(vmem_limit_bytes=32 << 20),
        name="conv_scores",
    )(canvas, top, bottom, side(left), side(right), weight, bias.reshape(1, hidden), readout.reshape(1, hidden))
    return out.reshape(height, breadth)


def spare_tiles(heads):
    return -(-3 * heads // 8)


def pack_rows(weight, groups):
    rows, cols = weight.shape
    eights = rows // 8
    kind_cols = cols // 3

    def body(w_ref, *outs):
        w = w_ref[...].astype(F32)
        zero = jnp.zeros((1, 128), F32)
        for (first, heads), out_ref in zip(groups, outs, strict=True):
            tiles = [kind * kind_cols + (first + h) * HD for kind in range(3) for h in range(heads)]
            spare = spare_tiles(heads)
            for j in range(spare):
                pieces = [w[rows - 1 : rows, t : t + 128] for t in tiles[8 * j : 8 * j + 8]]
                pieces += [zero] * (8 - len(pieces))
                out_ref[:, j * 128 : (j + 1) * 128] = jnp.concatenate(pieces, axis=0).astype(BF)
            for b in range(eights):
                for kind in range(3):
                    at = (spare + (3 * b + kind) * heads) * HD
                    low = kind * kind_cols + first * HD
                    out_ref[:, at : at + heads * HD] = w[8 * b : 8 * b + 8, low : low + heads * HD].astype(BF)

    return pl.pallas_call(
        body,
        out_shape=tuple(
            jax.ShapeDtypeStruct((8, (spare_tiles(heads) + 3 * eights * heads) * HD), BF) for _, heads in groups
        ),
        in_specs=[VMEM],
        out_specs=tuple(VMEM for _ in groups),
        name="pack_rows",
    )(weight)


def project_and_attend(before, here, after, packed, sharp, own_ids, key_ids, first, heads, cores_apart, partial):
    rows, width = here.shape
    deep = packed.shape[0]
    eights, parts = width // deep, deep // 8
    near = 3 * rows
    spare = spare_tiles(heads)
    scale = 1.0 / math.sqrt(HD)
    span = 256

    def body(xb, xh, xa, ext, *refs):
        w_refs = refs[:9]
        sharp_ref, own_ref, key_ref = refs[9:12]
        out_ref, x, bias, wide, lasts, q_buf, k_buf, v_buf = refs[-8:]
        n = pl.program_id(0)
        head = jnp.minimum(n, heads - 1)

        @pl.when(n == 0)
        def _():
            x[0:rows] = xb[...]
            x[rows : 2 * rows] = xh[...]
            x[2 * rows :] = xa[...]
            if cores_apart:
                came = lax.broadcasted_iota(jnp.int32, (span, span), 0)
                went = lax.broadcasted_iota(jnp.int32, (span, span), 1)
                half = span // 2
                core, rest = went // half, went % half
                swap = jnp.where(came == (rest // 8) * 16 + core * 8 + rest % 8, 1.0, 0.0).astype(BF)
                for at in range(0, eights * deep, span):
                    x[:, at : at + span] = jnp.dot(
                        x[:, at : at + span], swap, preferred_element_type=F32
                    ).astype(BF)
                low = eights * deep
                x[:, low:] = jnp.dot(x[:, low:], lane_swap(parts), preferred_element_type=F32).astype(BF)
            bias[...] = jnp.where(own_ref[...] == key_ref[...], 0.0, -1e30)
            for j in range(spare):
                wide[j] = ext[:, j * 128 : (j + 1) * 128].astype(F32)
            for j in range(spare):
                for s in range(8):
                    lasts[8 * j + s] = wide[j, pl.ds(s, parts, stride=8), :].astype(BF)
            q_buf[1] = jnp.zeros((rows, HD), BF)
            k_buf[1] = jnp.zeros((near, HD), BF)
            v_buf[1] = jnp.zeros((near, HD), BF)

        done = (n + 1) % 2
        logits = lax.dot_general(
            q_buf[done], k_buf[done], (((1,), (1,)), ((), ())), preferred_element_type=F32
        )
        logits = logits * scale + bias[...]
        peak = jnp.max(logits, axis=1, keepdims=True)
        weights = jnp.exp(logits - peak)
        total = jnp.sum(weights, axis=1, keepdims=True)
        result = jnp.dot(weights.astype(BF), v_buf[done], preferred_element_type=F32)
        out_ref[...] = (result / total).astype(BF)

        q = jnp.zeros((rows, HD), F32)
        kv = jnp.zeros((near, 2 * HD), F32)
        for b in range(eights):
            at = b * deep
            q = q + jnp.dot(x[rows : 2 * rows, at : at + deep], w_refs[b][...], preferred_element_type=F32)
            both = jnp.concatenate([w_refs[3 + b][...], w_refs[6 + b][...]], axis=1)
            kv = kv + jnp.dot(x[:, at : at + deep], both, preferred_element_type=F32)
        at = eights * deep
        q = q + jnp.dot(x[rows : 2 * rows, at:], lasts[head], preferred_element_type=F32)
        both = jnp.concatenate([lasts[head + heads], lasts[head + 2 * heads]], axis=1)
        kv = kv + jnp.dot(x[:, at:], both, preferred_element_type=F32)
        new = n % 2
        q_buf[new] = q.astype(BF)
        k_buf[new] = (kv[:, :HD] * sharp_ref[...]).astype(BF)
        v_buf[new] = kv[:, HD:].astype(BF)

    def lane_swap(size):
        came = lax.broadcasted_iota(jnp.int32, (size, size), 0)
        went = lax.broadcasted_iota(jnp.int32, (size, size), 1)
        line, core, rest = went // 32, (went % 32) // 16, went % 16
        return jnp.where(came == line * 32 + rest * 2 + core, 1.0, 0.0).astype(BF)

    def w_spec(b, kind):
        base = spare + (3 * b + kind) * heads
        return pl.BlockSpec((deep, HD), lambda n: (0, base + jnp.minimum(n, heads - 1)))

    extra = [] if partial is None else [partial]
    return pl.pallas_call(
        body,
        grid=(heads + 1,),
        out_shape=jax.ShapeDtypeStruct((rows, HW), BF),
        in_specs=[VMEM, VMEM, VMEM, pl.BlockSpec((deep, spare * 128), lambda n: (0, 0))]
        + [w_spec(b, kind) for kind in range(3) for b in range(3)]
        + [VMEM, VMEM, VMEM]
        + [ANY for _ in extra],
        out_specs=pl.BlockSpec((rows, HD), lambda n: (0, first + jnp.maximum(n - 1, 0))),
        input_output_aliases={16: 0} if extra else {},
        scratch_shapes=[
            pltpu.VMEM((near, width), BF),
            pltpu.VMEM((rows, near), F32),
            pltpu.VMEM((spare, deep, 128), F32),
            pltpu.VMEM((8 * spare, parts, HD), BF),
            pltpu.VMEM((2, rows, HD), BF),
            pltpu.VMEM((2, near, HD), BF),
            pltpu.VMEM((2, near, HD), BF),
        ],
        compiler_params=pltpu.CompilerParams(vmem_limit_bytes=48 << 20),
        name="project_and_attend",
    )(before, here, after, *([packed] * 10), sharp, own_ids, key_ids, *extra)


def shards(
    canvas,
    conv_weight,
    conv_bias,
    score_weight,
    tile_tokens,
    tile_cell,
    tile_count,
    holder_order,
    tile_image,
    ln_gain,
    qkv_weight,
):
    axes = ("grp", "dev")
    holders = lax.axis_size("dev")
    parts = holders * lax.axis_size("grp")
    own = lax.axis_index("dev")
    counts, order = tile_count[0], holder_order[0]
    tile_len = tile_tokens.shape[1]
    held_rows = MT * tile_len

    sent = send_order(counts, order, own.reshape(1), tile_tokens)
    recv = lax.all_to_all(sent, "dev", split_axis=0, concat_axis=0, tiled=True)

    near_heads, far_heads = (FIRST, HEADS - FIRST), (0, FIRST)
    near_rows, far_rows = pack_rows(qkv_weight, (near_heads, far_heads))
    far_packed = lax.all_gather(far_rows, axes, axis=0, tiled=True)
    near_packed = gather_rows(near_rows)

    up, down = ring_pairs("grp")
    top = lax.ppermute(canvas[-1:], "grp", up)
    bottom = lax.ppermute(canvas[:1], "grp", down)
    up, down = ring_pairs("dev")

    def edge(col):
        return jnp.concatenate([top[:, col], canvas[:, col], bottom[:, col]], axis=0)

    left = lax.ppermute(edge(-1), "dev", up)
    right = lax.ppermute(edge(0), "dev", down)
    score_map = conv_scores(canvas, top, bottom, left, right, conv_weight, conv_bias, score_weight)

    ranks = jnp.arange(holders, dtype=jnp.int32)
    first = jnp.sum(jnp.where(ranks < own, counts, 0))
    place_of = jnp.sum(jnp.where(order[None, :] == ranks[:, None], ranks[None, :], 0), axis=1)
    slot_for = (place_of - first) & (holders - 1)
    cells = jnp.take(tile_cell[0], slot_for)
    send_score = jnp.take(score_map.reshape(-1), cells).astype(BF)
    send_score = jnp.stack([jnp.roll(send_score, 1), send_score, jnp.roll(send_score, -1)], axis=1)
    recv, send_score = lax.optimization_barrier((recv, send_score))
    recv_score = lax.all_to_all(send_score, "dev", split_axis=0, concat_axis=0, tiled=True)

    near_holders = jnp.clip(own + jnp.arange(-1, 2, dtype=jnp.int32), 0, holders - 1)
    places = jnp.sum(jnp.where(order[None, :] == near_holders[:, None], ranks[None, :], 0), axis=1)
    wanted = jnp.arange(MT, dtype=jnp.int32)[None, :] * holders + places[:, None]
    ends = jnp.sum(jnp.where(ranks[None, :] <= ranks[:, None], counts[None, :], 0), axis=1)
    source = jnp.sum((ends <= wanted[:, :, None]).astype(jnp.int32), axis=2)
    picked = source[:, :, None] == ranks
    near_score = jnp.sum(jnp.where(picked, recv_score.astype(F32).T[:, None, :], 0.0), axis=2)
    sharp = jnp.repeat(0.5 + jax.nn.softplus(near_score.reshape(-1)), tile_len)[:, None]

    here = hold_and_norm(source[1], recv, ln_gain, parts)
    before = lax.ppermute(here, "dev", up)
    after = lax.ppermute(here, "dev", down)

    all_ids = tile_image[0]
    places = own * MT - MT + jnp.arange(3 * MT, dtype=jnp.int32)
    inside = (places >= 0) & (places < all_ids.shape[0])
    near_ids = jnp.where(inside, jnp.take(all_ids, jnp.clip(places, 0, all_ids.shape[0] - 1)), -1)
    key_ids = jnp.repeat(near_ids, tile_len)
    own_ids = key_ids[held_rows : 2 * held_rows]
    rest = (sharp, own_ids[:, None], key_ids[None, :])
    attended = project_and_attend(before, here, after, near_packed, *rest, *near_heads, True, None)
    attended = project_and_attend(before, here, after, far_packed, *rest, *far_heads, False, attended)
    return (score_map, attended)


def solution(mesh):
    placed = (
        P("grp", "dev", None),
        P(),
        P(),
        P(),
        P(("grp", "dev"), None, None),
        P("grp", "dev"),
        P("grp", None),
        P("grp", None),
        P("grp", None),
        P(),
        P(("grp", "dev"), None),
    )
    return jax.shard_map(
        shards,
        mesh=mesh,
        in_specs=placed,
        out_specs=(P("grp", "dev"), P(("grp", "dev"), None)),
        check_vma=False,
    )
```

```python
import math

import jax
import jax.numpy as jnp
import numpy as np
from jax import lax
from jax.experimental import pallas as pl
from jax.experimental.pallas import tpu as pltpu
from jax.sharding import PartitionSpec as P


HD = 128
HEADS = 13
HW = HEADS * HD
MT = 8
BF = jnp.bfloat16
F32 = jnp.float32
ANY = pl.BlockSpec(memory_space=pl.ANY)
SMEM = pl.BlockSpec(memory_space=pltpu.SMEM)
VMEM = pl.BlockSpec(memory_space=pltpu.VMEM)


def ring_pairs(axis):
    size = lax.axis_size(axis)
    up = [(i, i + 1) for i in range(size - 1)]
    return up, [(j, i) for i, j in up]


def send_order(counts, order, own, tokens):
    holders = order.shape[0]

    def body(counts_ref, order_ref, own_ref, tok_ref, out_ref, tiles, in_sems, out_sems):
        fetch = [pltpu.make_async_copy(tok_ref.at[s], tiles.at[s], in_sems.at[s]) for s in range(holders)]
        for c in fetch:
            c.start()
        first = lax.fori_loop(0, own_ref[0], lambda j, acc: acc + counts_ref[j], jnp.int32(0))

        def copy(s):
            holder = order_ref[(first + s) & (holders - 1)]
            return pltpu.make_async_copy(tiles.at[s], out_ref.at[holder], out_sems.at[s])

        for s in range(holders):
            fetch[s].wait()
            copy(s).start()
        for s in range(holders):
            copy(s).wait()

    return pl.pallas_call(
        body,
        out_shape=jax.ShapeDtypeStruct(tokens.shape, tokens.dtype),
        in_specs=[SMEM, SMEM, SMEM, ANY],
        out_specs=ANY,
        scratch_shapes=[
            pltpu.VMEM(tokens.shape, tokens.dtype),
            pltpu.SemaphoreType.DMA((holders,)),
            pltpu.SemaphoreType.DMA((holders,)),
        ],
        name="send_order",
    )(counts, order, own, tokens)


def spread_index(parts, rows):
    part, row = np.arange(parts)[:, None], np.arange(8)[None, :]
    main = [(rows * part + 8 * b + row).reshape(-1) for b in range(rows // 8)]
    return np.concatenate(main + [rows * np.arange(parts) + rows - 1]).astype(np.int32)


def hold_and_norm(source, recv, gain, parts):
    tile_len, width = recv.shape[1], recv.shape[2]
    rows = MT * tile_len
    index = spread_index(parts, width // parts)
    blocks = width // 128
    table = jnp.asarray(index.reshape(blocks, 128))

    def body(src_ref, recv_ref, gain_ref, table_ref, out_ref, tiles, normed, sems):
        copies = [
            pltpu.make_async_copy(recv_ref.at[src_ref[m]], tiles.at[m], sems.at[m]) for m in range(MT)
        ]
        for c in copies:
            c.start()
        for m in range(MT):
            copies[m].wait()
            values = tiles[m].astype(F32)
            center = jnp.mean(values, axis=1, keepdims=True)
            values = values - center
            spread = jnp.mean(values * values, axis=1, keepdims=True)
            scaled = values * lax.rsqrt(spread + 1e-06) * gain_ref[...]
            normed[m * tile_len : (m + 1) * tile_len, :] = scaled.astype(BF)
        for n in range(blocks):
            part = index[n * 128 : (n + 1) * 128]
            low = int(part.min()) // 128 * 128
            high = int(part.max()) // 128 * 128 + 128
            place = lax.broadcasted_iota(jnp.int32, (high - low, 128), 0) + low
            pick = jnp.where(place == table_ref[n : n + 1, :], 1.0, 0.0).astype(BF)
            out_ref[:, n * 128 : (n + 1) * 128] = jnp.dot(
                normed[:, low:high], pick, preferred_element_type=F32
            ).astype(BF)

    return pl.pallas_call(
        body,
        out_shape=jax.ShapeDtypeStruct((rows, width), BF),
        in_specs=[SMEM, ANY, VMEM, VMEM],
        out_specs=VMEM,
        scratch_shapes=[
            pltpu.VMEM((MT, tile_len, width), BF),
            pltpu.VMEM((rows, width), BF),
            pltpu.SemaphoreType.DMA((MT,)),
        ],
        name="hold_and_norm",
    )(source, recv, gain.reshape(1, width), table)


def conv_scores(canvas, top, bottom, left, right, weight, bias, readout):
    height, breadth, channels = canvas.shape
    hidden = weight.shape[1]
    step = 8
    pixels = step * breadth

    def side(edge):
        return jnp.concatenate([edge[0:height], edge[1 : height + 1], edge[2 : height + 2]], axis=1)

    def body(canvas_ref, top_ref, bottom_ref, left_ref, right_ref, w_ref, bias_ref, read_ref, out_ref,
             padded, lside, rside, sem):
        i = pl.program_id(0)

        def w_of(col):
            return jnp.concatenate(
                [w_ref[(row * 3 + col) * channels : (row * 3 + col + 1) * channels, :] for row in range(3)],
                axis=0,
            )

        @pl.when(i == 0)
        def _():
            fetch = pltpu.make_async_copy(canvas_ref, padded.at[pl.ds(1, height)], sem)
            fetch.start()
            padded[0:1] = top_ref[...]
            padded[height + 1 : height + 2] = bottom_ref[...]
            sides = (height // step, step, hidden)
            lside[...] = jnp.dot(left_ref[...], w_of(0), preferred_element_type=F32).reshape(sides)
            rside[...] = jnp.dot(right_ref[...], w_of(2), preferred_element_type=F32).reshape(sides)
            fetch.wait()

        window = jnp.concatenate(
            [padded[pl.ds(i * step + row, step)].reshape(pixels, channels) for row in range(3)], axis=1
        )
        before = jnp.dot(window, w_of(0), preferred_element_type=F32)
        at = jnp.dot(window, w_of(1), preferred_element_type=F32)
        after = jnp.dot(window, w_of(2), preferred_element_type=F32)
        before = pltpu.roll(before, 1, 0).reshape(step, breadth, hidden)
        after = pltpu.roll(after, pixels - 1, 0).reshape(step, breadth, hidden)
        col = lax.broadcasted_iota(jnp.int32, (step, breadth, hidden), 1)
        lrow = lside[i]
        rrow = rside[i]
        before = jnp.where(col == 0, lrow[:, None, :], before)
        after = jnp.where(col == breadth - 1, rrow[:, None, :], after)
        x = (before + after).reshape(pixels, hidden) + at + bias_ref[...]
        inner = math.sqrt(2.0 / math.pi) * (x + 0.044715 * (x * x * x))
        h = x * (0.5 * (1.0 + jnp.tanh(inner)))
        h = h * read_ref[...]
        half = h[:, 0:128]
        for k in range(1, hidden // 128):
            half = half + h[:, k * 128 : (k + 1) * 128]
        ones = jnp.ones((8, 128), F32)
        score = lax.dot_general(
            ones, half, (((1,), (1,)), ((), ())), precision=lax.Precision.HIGHEST, preferred_element_type=F32
        )
        for r in range(step):
            out_ref[0, r : r + 1, :] = score[0:1, r * breadth : (r + 1) * breadth]

    out = pl.pallas_call(
        body,
        grid=(height // step,),
        out_shape=jax.ShapeDtypeStruct((height // step, step, breadth), F32),
        in_specs=[ANY] + [pl.BlockSpec(memory_space=pltpu.VMEM)] * 7,
        out_specs=pl.BlockSpec((1, step, breadth), lambda i: (i, 0, 0)),
        scratch_shapes=[
            pltpu.VMEM((height + 2, breadth, channels), BF),
            pltpu.VMEM((height // step, step, hidden), F32),
            pltpu.VMEM((height // step, step, hidden), F32),
            pltpu.SemaphoreType.DMA,
        ],
        compiler_params=pltpu.CompilerParams(vmem_limit_bytes=32 << 20),
        name="conv_scores",
    )(canvas, top, bottom, side(left), side(right), weight, bias.reshape(1, hidden), readout.reshape(1, hidden))
    return out.reshape(height, breadth)


def pack_rows(weight):
    rows, cols = weight.shape
    eights, tiles = rows // 8, cols // 128
    spare = -(-tiles // 8)

    def body(w_ref, out_ref):
        w = w_ref[...].astype(F32)
        zero = jnp.zeros((1, 128), F32)
        for j in range(spare):
            pieces = [
                w[rows - 1 : rows, t * 128 : (t + 1) * 128] if t < tiles else zero
                for t in range(8 * j, 8 * j + 8)
            ]
            out_ref[:, j * 128 : (j + 1) * 128] = jnp.concatenate(pieces, axis=0).astype(BF)
        for b in range(eights):
            at = spare * 128 + b * cols
            out_ref[:, at : at + cols] = w[8 * b : 8 * b + 8].astype(BF)

    return pl.pallas_call(
        body,
        out_shape=jax.ShapeDtypeStruct((8, spare * 128 + eights * cols), BF),
        in_specs=[VMEM],
        out_specs=VMEM,
        name="pack_rows",
    )(weight)


def project_and_attend(before, here, after, packed, sharp, own_ids, key_ids):
    rows, width = here.shape
    deep = packed.shape[0]
    eights, parts = width // deep, deep // 8
    near = 3 * rows
    spare = -(-3 * HEADS // 8)
    scale = 1.0 / math.sqrt(HD)

    def body(xb, xh, xa, ext, *refs):
        w_refs = (refs[:9], refs[9:18])
        sharp_ref, own_ref, key_ref, out_ref, x, bias, wide, lasts, q_buf, k_buf, v_buf = refs[18:]
        n = pl.program_id(0)
        heads = [jnp.minimum(2 * n + slot, HEADS - 1) for slot in range(2)]

        @pl.when(n == 0)
        def _():
            x[0:rows] = xb[...]
            x[rows : 2 * rows] = xh[...]
            x[2 * rows :] = xa[...]
            bias[...] = jnp.where(own_ref[...] == key_ref[...], 0.0, -1e30)
            for j in range(spare):
                wide[j] = ext[:, j * 128 : (j + 1) * 128].astype(F32)
            for j in range(spare):
                for s in range(8):
                    lasts[8 * j + s] = wide[j, pl.ds(s, parts, stride=8), :].astype(BF)
            q_buf[1] = jnp.zeros((2, rows, HD), BF)
            k_buf[1] = jnp.zeros((2, near, HD), BF)
            v_buf[1] = jnp.zeros((2, near, HD), BF)

        done, new = (n + 1) % 2, n % 2
        for slot in range(2):
            logits = lax.dot_general(
                q_buf[done, slot], k_buf[done, slot], (((1,), (1,)), ((), ())), preferred_element_type=F32
            )
            logits = logits * scale + bias[...]
            peak = jnp.max(logits, axis=1, keepdims=True)
            weights = jnp.exp(logits - peak)
            total = jnp.sum(weights, axis=1, keepdims=True)
            result = jnp.dot(weights.astype(BF), v_buf[done, slot], preferred_element_type=F32)
            out_ref[:, slot * HD : (slot + 1) * HD] = (result / total).astype(BF)

        at = eights * deep
        q = jnp.dot(
            xh[:, at:], jnp.concatenate([lasts[h] for h in heads], axis=1), preferred_element_type=F32
        )
        for b in range(eights):
            both = jnp.concatenate([w_refs[0][b][...], w_refs[1][b][...]], axis=1)
            q = q + jnp.dot(xh[:, b * deep : (b + 1) * deep], both, preferred_element_type=F32)
        for slot in range(2):
            q_buf[new, slot] = q[:, slot * HD : (slot + 1) * HD].astype(BF)
            h = heads[slot]
            both = jnp.concatenate([lasts[h + HEADS], lasts[h + 2 * HEADS]], axis=1)
            kv = jnp.dot(x[:, at:], both, preferred_element_type=F32)
            for b in range(eights):
                both = jnp.concatenate([w_refs[slot][3 + b][...], w_refs[slot][6 + b][...]], axis=1)
                kv = kv + jnp.dot(x[:, b * deep : (b + 1) * deep], both, preferred_element_type=F32)
            k_buf[new, slot] = (kv[:, :HD] * sharp_ref[...]).astype(BF)
            v_buf[new, slot] = kv[:, HD:].astype(BF)

    def w_spec(b, kind, slot):
        first = spare + b * 3 * HEADS + kind * HEADS
        return pl.BlockSpec((deep, HD), lambda n: (0, first + jnp.minimum(2 * n + slot, HEADS - 1)))

    return pl.pallas_call(
        body,
        grid=(-(-HEADS // 2) + 1,),
        out_shape=jax.ShapeDtypeStruct((rows, HW), BF),
        in_specs=[VMEM, VMEM, VMEM, pl.BlockSpec((deep, spare * 128), lambda n: (0, 0))]
        + [w_spec(b, kind, slot) for slot in range(2) for kind in range(3) for b in range(3)]
        + [VMEM, VMEM, VMEM],
        out_specs=pl.BlockSpec((rows, 2 * HD), lambda n: (0, jnp.maximum(n - 1, 0))),
        scratch_shapes=[
            pltpu.VMEM((near, width), BF),
            pltpu.VMEM((rows, near), F32),
            pltpu.VMEM((spare, deep, 128), F32),
            pltpu.VMEM((8 * spare, parts, HD), BF),
            pltpu.VMEM((2, 2, rows, HD), BF),
            pltpu.VMEM((2, 2, near, HD), BF),
            pltpu.VMEM((2, 2, near, HD), BF),
        ],
        compiler_params=pltpu.CompilerParams(vmem_limit_bytes=48 << 20),
        name="project_and_attend",
    )(before, here, after, *([packed] * 19), sharp, own_ids, key_ids)


def shards(
    canvas,
    conv_weight,
    conv_bias,
    score_weight,
    tile_tokens,
    tile_cell,
    tile_count,
    holder_order,
    tile_image,
    ln_gain,
    qkv_weight,
):
    axes = ("grp", "dev")
    holders = lax.axis_size("dev")
    parts = holders * lax.axis_size("grp")
    own = lax.axis_index("dev")
    counts, order = tile_count[0], holder_order[0]
    tile_len = tile_tokens.shape[1]
    held_rows = MT * tile_len

    sent = send_order(counts, order, own.reshape(1), tile_tokens)
    recv = lax.all_to_all(sent, "dev", split_axis=0, concat_axis=0, tiled=True)

    packed = lax.all_gather(pack_rows(qkv_weight), axes, axis=0, tiled=True)

    up, down = ring_pairs("grp")
    top = lax.ppermute(canvas[-1:], "grp", up)
    bottom = lax.ppermute(canvas[:1], "grp", down)
    up, down = ring_pairs("dev")

    def edge(col):
        return jnp.concatenate([top[:, col], canvas[:, col], bottom[:, col]], axis=0)

    left = lax.ppermute(edge(-1), "dev", up)
    right = lax.ppermute(edge(0), "dev", down)
    score_map = conv_scores(canvas, top, bottom, left, right, conv_weight, conv_bias, score_weight)

    ranks = jnp.arange(holders, dtype=jnp.int32)
    first = jnp.sum(jnp.where(ranks < own, counts, 0))
    place_of = jnp.sum(jnp.where(order[None, :] == ranks[:, None], ranks[None, :], 0), axis=1)
    slot_for = (place_of - first) & (holders - 1)
    cells = jnp.take(tile_cell[0], slot_for)
    send_score = jnp.take(score_map.reshape(-1), cells).astype(BF)
    send_score = jnp.stack([jnp.roll(send_score, 1), send_score, jnp.roll(send_score, -1)], axis=1)
    _, send_score = lax.optimization_barrier((recv, send_score))
    recv_score = lax.all_to_all(send_score, "dev", split_axis=0, concat_axis=0, tiled=True)

    near_holders = jnp.clip(own + jnp.arange(-1, 2, dtype=jnp.int32), 0, holders - 1)
    places = jnp.sum(jnp.where(order[None, :] == near_holders[:, None], ranks[None, :], 0), axis=1)
    wanted = jnp.arange(MT, dtype=jnp.int32)[None, :] * holders + places[:, None]
    ends = jnp.sum(jnp.where(ranks[None, :] <= ranks[:, None], counts[None, :], 0), axis=1)
    source = jnp.sum((ends <= wanted[:, :, None]).astype(jnp.int32), axis=2)
    picked = source[:, :, None] == ranks
    near_score = jnp.sum(jnp.where(picked, recv_score.astype(F32).T[:, None, :], 0.0), axis=2)
    sharp = jnp.repeat(0.5 + jax.nn.softplus(near_score.reshape(-1)), tile_len)[:, None]

    here = hold_and_norm(source[1], recv, ln_gain, parts)
    before = lax.ppermute(here, "dev", up)
    after = lax.ppermute(here, "dev", down)

    all_ids = tile_image[0]
    places = own * MT - MT + jnp.arange(3 * MT, dtype=jnp.int32)
    inside = (places >= 0) & (places < all_ids.shape[0])
    near_ids = jnp.where(inside, jnp.take(all_ids, jnp.clip(places, 0, all_ids.shape[0] - 1)), -1)
    key_ids = jnp.repeat(near_ids, tile_len)
    own_ids = key_ids[held_rows : 2 * held_rows]
    attended = project_and_attend(before, here, after, packed, sharp, own_ids[:, None], key_ids[None, :])
    return (score_map, attended)


def solution(mesh):
    placed = (
        P("grp", "dev", None),
        P(),
        P(),
        P(),
        P(("grp", "dev"), None, None),
        P("grp", "dev"),
        P("grp", None),
        P("grp", None),
        P("grp", None),
        P(),
        P(("grp", "dev"), None),
    )
    return jax.shard_map(
        shards,
        mesh=mesh,
        in_specs=placed,
        out_specs=(P("grp", "dev"), P(("grp", "dev"), None)),
        check_vma=False,
    )
```

```python
import math

import jax
import jax.numpy as jnp
import numpy as np
from jax import lax
from jax.experimental import pallas as pl
from jax.experimental.pallas import tpu as pltpu
from jax.sharding import PartitionSpec as P


HD = 128
HEADS = 13
HW = HEADS * HD
MT = 8
BF = jnp.bfloat16
F32 = jnp.float32
ANY = pl.BlockSpec(memory_space=pl.ANY)
SMEM = pl.BlockSpec(memory_space=pltpu.SMEM)
VMEM = pl.BlockSpec(memory_space=pltpu.VMEM)


def ring_pairs(axis):
    size = lax.axis_size(axis)
    up = [(i, i + 1) for i in range(size - 1)]
    return up, [(j, i) for i, j in up]


def send_order(counts, order, own, tokens):
    holders = order.shape[0]

    def body(counts_ref, order_ref, own_ref, tok_ref, out_ref, tiles, in_sems, out_sems):
        fetch = [pltpu.make_async_copy(tok_ref.at[s], tiles.at[s], in_sems.at[s]) for s in range(holders)]
        for c in fetch:
            c.start()
        first = lax.fori_loop(0, own_ref[0], lambda j, acc: acc + counts_ref[j], jnp.int32(0))

        def copy(s):
            holder = order_ref[(first + s) & (holders - 1)]
            return pltpu.make_async_copy(tiles.at[s], out_ref.at[holder], out_sems.at[s])

        for s in range(holders):
            fetch[s].wait()
            copy(s).start()
        for s in range(holders):
            copy(s).wait()

    return pl.pallas_call(
        body,
        out_shape=jax.ShapeDtypeStruct(tokens.shape, tokens.dtype),
        in_specs=[SMEM, SMEM, SMEM, ANY],
        out_specs=ANY,
        scratch_shapes=[
            pltpu.VMEM(tokens.shape, tokens.dtype),
            pltpu.SemaphoreType.DMA((holders,)),
            pltpu.SemaphoreType.DMA((holders,)),
        ],
        name="send_order",
    )(counts, order, own, tokens)


def spread_index(parts, rows):
    part, row = np.arange(parts)[:, None], np.arange(8)[None, :]
    main = [(rows * part + 8 * b + row).reshape(-1) for b in range(rows // 8)]
    return np.concatenate(main + [rows * np.arange(parts) + rows - 1]).astype(np.int32)


def hold_and_norm(source, recv, gain, parts):
    tile_len, width = recv.shape[1], recv.shape[2]
    rows = MT * tile_len
    index = spread_index(parts, width // parts)
    blocks = width // 128
    table = jnp.asarray(index.reshape(blocks, 128))

    def body(src_ref, recv_ref, gain_ref, table_ref, out_ref, tiles, normed, sems):
        copies = [
            pltpu.make_async_copy(recv_ref.at[src_ref[m]], tiles.at[m], sems.at[m]) for m in range(MT)
        ]
        for c in copies:
            c.start()
        for m in range(MT):
            copies[m].wait()
            values = tiles[m].astype(F32)
            center = jnp.mean(values, axis=1, keepdims=True)
            values = values - center
            spread = jnp.mean(values * values, axis=1, keepdims=True)
            scaled = values * lax.rsqrt(spread + 1e-06) * gain_ref[...]
            normed[m * tile_len : (m + 1) * tile_len, :] = scaled.astype(BF)
        for n in range(blocks):
            part = index[n * 128 : (n + 1) * 128]
            low = int(part.min()) // 128 * 128
            high = int(part.max()) // 128 * 128 + 128
            place = lax.broadcasted_iota(jnp.int32, (high - low, 128), 0) + low
            pick = jnp.where(place == table_ref[n : n + 1, :], 1.0, 0.0).astype(BF)
            out_ref[:, n * 128 : (n + 1) * 128] = jnp.dot(
                normed[:, low:high], pick, preferred_element_type=F32
            ).astype(BF)

    return pl.pallas_call(
        body,
        out_shape=jax.ShapeDtypeStruct((rows, width), BF),
        in_specs=[SMEM, ANY, VMEM, VMEM],
        out_specs=VMEM,
        scratch_shapes=[
            pltpu.VMEM((MT, tile_len, width), BF),
            pltpu.VMEM((rows, width), BF),
            pltpu.SemaphoreType.DMA((MT,)),
        ],
        name="hold_and_norm",
    )(source, recv, gain.reshape(1, width), table)


def conv_scores(canvas, top, bottom, left, right, weight, bias, readout):
    height, breadth, channels = canvas.shape
    hidden = weight.shape[1]
    step = 8
    pixels = step * breadth

    def side(edge):
        return jnp.concatenate([edge[0:height], edge[1 : height + 1], edge[2 : height + 2]], axis=1)

    def body(canvas_ref, top_ref, bottom_ref, left_ref, right_ref, w_ref, bias_ref, read_ref, out_ref,
             padded, lside, rside, sem):
        i = pl.program_id(0)

        def w_of(col):
            return jnp.concatenate(
                [w_ref[(row * 3 + col) * channels : (row * 3 + col + 1) * channels, :] for row in range(3)],
                axis=0,
            )

        @pl.when(i == 0)
        def _():
            fetch = pltpu.make_async_copy(canvas_ref, padded.at[pl.ds(1, height)], sem)
            fetch.start()
            padded[0:1] = top_ref[...]
            padded[height + 1 : height + 2] = bottom_ref[...]
            sides = (height // step, step, hidden)
            lside[...] = jnp.dot(left_ref[...], w_of(0), preferred_element_type=F32).reshape(sides)
            rside[...] = jnp.dot(right_ref[...], w_of(2), preferred_element_type=F32).reshape(sides)
            fetch.wait()

        window = jnp.concatenate(
            [padded[pl.ds(i * step + row, step)].reshape(pixels, channels) for row in range(3)], axis=1
        )
        before = jnp.dot(window, w_of(0), preferred_element_type=F32)
        at = jnp.dot(window, w_of(1), preferred_element_type=F32)
        after = jnp.dot(window, w_of(2), preferred_element_type=F32)
        before = pltpu.roll(before, 1, 0).reshape(step, breadth, hidden)
        after = pltpu.roll(after, pixels - 1, 0).reshape(step, breadth, hidden)
        col = lax.broadcasted_iota(jnp.int32, (step, breadth, hidden), 1)
        lrow = lside[i]
        rrow = rside[i]
        before = jnp.where(col == 0, lrow[:, None, :], before)
        after = jnp.where(col == breadth - 1, rrow[:, None, :], after)
        x = (before + after).reshape(pixels, hidden) + at + bias_ref[...]
        inner = math.sqrt(2.0 / math.pi) * (x + 0.044715 * (x * x * x))
        h = x * (0.5 * (1.0 + jnp.tanh(inner)))
        h = h * read_ref[...]
        half = h[:, 0:128]
        for k in range(1, hidden // 128):
            half = half + h[:, k * 128 : (k + 1) * 128]
        ones = jnp.ones((8, 128), F32)
        score = lax.dot_general(
            ones, half, (((1,), (1,)), ((), ())), precision=lax.Precision.HIGHEST, preferred_element_type=F32
        )
        for r in range(step):
            out_ref[0, r : r + 1, :] = score[0:1, r * breadth : (r + 1) * breadth]

    out = pl.pallas_call(
        body,
        grid=(height // step,),
        out_shape=jax.ShapeDtypeStruct((height // step, step, breadth), F32),
        in_specs=[ANY] + [pl.BlockSpec(memory_space=pltpu.VMEM)] * 7,
        out_specs=pl.BlockSpec((1, step, breadth), lambda i: (i, 0, 0)),
        scratch_shapes=[
            pltpu.VMEM((height + 2, breadth, channels), BF),
            pltpu.VMEM((height // step, step, hidden), F32),
            pltpu.VMEM((height // step, step, hidden), F32),
            pltpu.SemaphoreType.DMA,
        ],
        compiler_params=pltpu.CompilerParams(vmem_limit_bytes=32 << 20),
        name="conv_scores",
    )(canvas, top, bottom, side(left), side(right), weight, bias.reshape(1, hidden), readout.reshape(1, hidden))
    return out.reshape(height, breadth)


def pack_rows(weight):
    rows, cols = weight.shape
    eights, tiles = rows // 8, cols // 128
    spare = -(-tiles // 8)

    def body(w_ref, out_ref):
        w = w_ref[...].astype(F32)
        zero = jnp.zeros((1, 128), F32)
        for j in range(spare):
            pieces = [
                w[rows - 1 : rows, t * 128 : (t + 1) * 128] if t < tiles else zero
                for t in range(8 * j, 8 * j + 8)
            ]
            out_ref[:, j * 128 : (j + 1) * 128] = jnp.concatenate(pieces, axis=0).astype(BF)
        for b in range(eights):
            at = spare * 128 + b * cols
            out_ref[:, at : at + cols] = w[8 * b : 8 * b + 8].astype(BF)

    return pl.pallas_call(
        body,
        out_shape=jax.ShapeDtypeStruct((8, spare * 128 + eights * cols), BF),
        in_specs=[VMEM],
        out_specs=VMEM,
        name="pack_rows",
    )(weight)


def project_and_attend(near_tokens, bias, packed, sharp):
    near, width = near_tokens.shape
    rows = near // 3
    deep = packed.shape[0]
    eights, parts = width // deep, deep // 8
    spare = -(-3 * HEADS // 8)
    scale = 1.0 / math.sqrt(HD)

    def body(x, bias, ext, *refs):
        w_refs = refs[:9]
        sharp_ref, out_ref, wide, lasts, q_buf, k_buf, v_buf = refs[9:]
        n = pl.program_id(0)
        head = jnp.minimum(n, HEADS - 1)

        @pl.when(n == 0)
        def _():
            for j in range(spare):
                wide[j] = ext[:, j * 128 : (j + 1) * 128].astype(F32)
            for j in range(spare):
                for s in range(8):
                    lasts[8 * j + s] = wide[j, pl.ds(s, parts, stride=8), :].astype(BF)
            q_buf[1] = jnp.zeros((rows, HD), BF)
            k_buf[1] = jnp.zeros((near, HD), BF)
            v_buf[1] = jnp.zeros((near, HD), BF)

        done = (n + 1) % 2
        logits = lax.dot_general(
            q_buf[done], k_buf[done], (((1,), (1,)), ((), ())), preferred_element_type=F32
        )
        logits = logits * scale + bias[...]
        peak = jnp.max(logits, axis=1, keepdims=True)
        weights = jnp.exp(logits - peak)
        total = jnp.sum(weights, axis=1, keepdims=True)
        result = jnp.dot(weights.astype(BF), v_buf[done], preferred_element_type=F32)
        out_ref[...] = (result / total).astype(BF)

        q = jnp.zeros((rows, HD), F32)
        kv = jnp.zeros((near, 2 * HD), F32)
        for b in range(eights):
            at = b * deep
            q = q + jnp.dot(x[rows : 2 * rows, at : at + deep], w_refs[b][...], preferred_element_type=F32)
            both = jnp.concatenate([w_refs[3 + b][...], w_refs[6 + b][...]], axis=1)
            kv = kv + jnp.dot(x[:, at : at + deep], both, preferred_element_type=F32)
        at = eights * deep
        q = q + jnp.dot(x[rows : 2 * rows, at:], lasts[head], preferred_element_type=F32)
        both = jnp.concatenate([lasts[head + HEADS], lasts[head + 2 * HEADS]], axis=1)
        kv = kv + jnp.dot(x[:, at:], both, preferred_element_type=F32)
        new = n % 2
        q_buf[new] = q.astype(BF)
        k_buf[new] = (kv[:, :HD] * sharp_ref[...]).astype(BF)
        v_buf[new] = kv[:, HD:].astype(BF)

    def w_spec(b, kind):
        first = spare + b * 3 * HEADS + kind * HEADS
        return pl.BlockSpec((deep, HD), lambda n: (0, first + jnp.minimum(n, HEADS - 1)))

    return pl.pallas_call(
        body,
        grid=(HEADS + 1,),
        out_shape=jax.ShapeDtypeStruct((rows, HW), BF),
        in_specs=[VMEM, VMEM, pl.BlockSpec((deep, spare * 128), lambda n: (0, 0))]
        + [w_spec(b, kind) for kind in range(3) for b in range(3)]
        + [VMEM],
        out_specs=pl.BlockSpec((rows, HD), lambda n: (0, jnp.maximum(n - 1, 0))),
        scratch_shapes=[
            pltpu.VMEM((spare, deep, 128), F32),
            pltpu.VMEM((8 * spare, parts, HD), BF),
            pltpu.VMEM((2, rows, HD), BF),
            pltpu.VMEM((2, near, HD), BF),
            pltpu.VMEM((2, near, HD), BF),
        ],
        compiler_params=pltpu.CompilerParams(vmem_limit_bytes=48 << 20),
        name="project_and_attend",
    )(near_tokens, bias, *([packed] * 10), sharp)


def shards(
    canvas,
    conv_weight,
    conv_bias,
    score_weight,
    tile_tokens,
    tile_cell,
    tile_count,
    holder_order,
    tile_image,
    ln_gain,
    qkv_weight,
):
    axes = ("grp", "dev")
    holders = lax.axis_size("dev")
    parts = holders * lax.axis_size("grp")
    own = lax.axis_index("dev")
    counts, order = tile_count[0], holder_order[0]
    tile_len = tile_tokens.shape[1]
    held_rows = MT * tile_len

    sent = send_order(counts, order, own.reshape(1), tile_tokens)
    recv = lax.all_to_all(sent, "dev", split_axis=0, concat_axis=0, tiled=True)

    packed = lax.all_gather(pack_rows(qkv_weight), axes, axis=0, tiled=True)

    up, down = ring_pairs("grp")
    top = lax.ppermute(canvas[-1:], "grp", up)
    bottom = lax.ppermute(canvas[:1], "grp", down)
    up, down = ring_pairs("dev")

    def edge(col):
        return jnp.concatenate([top[:, col], canvas[:, col], bottom[:, col]], axis=0)

    left = lax.ppermute(edge(-1), "dev", up)
    right = lax.ppermute(edge(0), "dev", down)
    score_map = conv_scores(canvas, top, bottom, left, right, conv_weight, conv_bias, score_weight)

    ranks = jnp.arange(holders, dtype=jnp.int32)
    first = jnp.sum(jnp.where(ranks < own, counts, 0))
    place_of = jnp.sum(jnp.where(order[None, :] == ranks[:, None], ranks[None, :], 0), axis=1)
    slot_for = (place_of - first) & (holders - 1)
    cells = jnp.take(tile_cell[0], slot_for)
    send_score = jnp.take(score_map.reshape(-1), cells).astype(BF)
    send_score = jnp.stack([jnp.roll(send_score, 1), send_score, jnp.roll(send_score, -1)], axis=1)
    _, send_score = lax.optimization_barrier((recv, send_score))
    recv_score = lax.all_to_all(send_score, "dev", split_axis=0, concat_axis=0, tiled=True)

    near_holders = jnp.clip(own + jnp.arange(-1, 2, dtype=jnp.int32), 0, holders - 1)
    places = jnp.sum(jnp.where(order[None, :] == near_holders[:, None], ranks[None, :], 0), axis=1)
    wanted = jnp.arange(MT, dtype=jnp.int32)[None, :] * holders + places[:, None]
    ends = jnp.sum(jnp.where(ranks[None, :] <= ranks[:, None], counts[None, :], 0), axis=1)
    source = jnp.sum((ends <= wanted[:, :, None]).astype(jnp.int32), axis=2)
    picked = source[:, :, None] == ranks
    near_score = jnp.sum(jnp.where(picked, recv_score.astype(F32).T[:, None, :], 0.0), axis=2)
    sharp = jnp.repeat(0.5 + jax.nn.softplus(near_score.reshape(-1)), tile_len)[:, None]

    here = hold_and_norm(source[1], recv, ln_gain, parts)
    before = lax.ppermute(here, "dev", up)
    after = lax.ppermute(here, "dev", down)

    all_ids = tile_image[0]
    places = own * MT - MT + jnp.arange(3 * MT, dtype=jnp.int32)
    inside = (places >= 0) & (places < all_ids.shape[0])
    near_ids = jnp.where(inside, jnp.take(all_ids, jnp.clip(places, 0, all_ids.shape[0] - 1)), -1)
    key_ids = jnp.repeat(near_ids, tile_len)
    own_ids = key_ids[held_rows : 2 * held_rows]
    near_tokens = jnp.concatenate([before, here, after], axis=0)
    bias = jnp.where(own_ids[:, None] == key_ids[None, :], 0.0, -1e30)
    attended = project_and_attend(near_tokens, bias, packed, sharp)
    return (score_map, attended)


def solution(mesh):
    placed = (
        P("grp", "dev", None),
        P(),
        P(),
        P(),
        P(("grp", "dev"), None, None),
        P("grp", "dev"),
        P("grp", None),
        P("grp", None),
        P("grp", None),
        P(),
        P(("grp", "dev"), None),
    )
    return jax.shard_map(
        shards,
        mesh=mesh,
        in_specs=placed,
        out_specs=(P("grp", "dev"), P(("grp", "dev"), None)),
        check_vma=False,
    )
```

```python
import math

import jax
import jax.numpy as jnp
import numpy as np
from jax import lax
from jax.experimental import pallas as pl
from jax.experimental.pallas import tpu as pltpu
from jax.sharding import PartitionSpec as P


HD = 128
HEADS = 13
HW = HEADS * HD
MT = 8
BF = jnp.bfloat16
F32 = jnp.float32
ANY = pl.BlockSpec(memory_space=pl.ANY)
SMEM = pl.BlockSpec(memory_space=pltpu.SMEM)
VMEM = pl.BlockSpec(memory_space=pltpu.VMEM)


def ring_pairs(axis):
    size = lax.axis_size(axis)
    up = [(i, i + 1) for i in range(size - 1)]
    return up, [(j, i) for i, j in up]


def send_order(counts, order, own, tokens):
    holders = order.shape[0]

    def body(counts_ref, order_ref, own_ref, tok_ref, out_ref, tiles, in_sems, out_sems):
        fetch = [pltpu.make_async_copy(tok_ref.at[s], tiles.at[s], in_sems.at[s]) for s in range(holders)]
        for c in fetch:
            c.start()
        first = lax.fori_loop(0, own_ref[0], lambda j, acc: acc + counts_ref[j], jnp.int32(0))

        def copy(s):
            holder = order_ref[(first + s) & (holders - 1)]
            return pltpu.make_async_copy(tiles.at[s], out_ref.at[holder], out_sems.at[s])

        for s in range(holders):
            fetch[s].wait()
            copy(s).start()
        for s in range(holders):
            copy(s).wait()

    return pl.pallas_call(
        body,
        out_shape=jax.ShapeDtypeStruct(tokens.shape, tokens.dtype),
        in_specs=[SMEM, SMEM, SMEM, ANY],
        out_specs=ANY,
        scratch_shapes=[
            pltpu.VMEM(tokens.shape, tokens.dtype),
            pltpu.SemaphoreType.DMA((holders,)),
            pltpu.SemaphoreType.DMA((holders,)),
        ],
        name="send_order",
    )(counts, order, own, tokens)


def spread_index(parts, rows):
    part, row = np.arange(parts)[:, None], np.arange(8)[None, :]
    main = [(rows * part + 8 * b + row).reshape(-1) for b in range(rows // 8)]
    return np.concatenate(main + [rows * np.arange(parts) + rows - 1]).astype(np.int32)


def hold_and_norm(source, recv, gain, parts):
    tile_len, width = recv.shape[1], recv.shape[2]
    rows = MT * tile_len
    index = spread_index(parts, width // parts)
    blocks = width // 128
    table = jnp.asarray(index.reshape(blocks, 128))

    def body(src_ref, recv_ref, gain_ref, table_ref, out_ref, tiles, normed, sems):
        copies = [
            pltpu.make_async_copy(recv_ref.at[src_ref[m]], tiles.at[m], sems.at[m]) for m in range(MT)
        ]
        for c in copies:
            c.start()
        for m in range(MT):
            copies[m].wait()
            values = tiles[m].astype(F32)
            center = jnp.mean(values, axis=1, keepdims=True)
            values = values - center
            spread = jnp.mean(values * values, axis=1, keepdims=True)
            scaled = values * lax.rsqrt(spread + 1e-06) * gain_ref[...]
            normed[m * tile_len : (m + 1) * tile_len, :] = scaled.astype(BF)
        for n in range(blocks):
            part = index[n * 128 : (n + 1) * 128]
            low = int(part.min()) // 128 * 128
            high = int(part.max()) // 128 * 128 + 128
            place = lax.broadcasted_iota(jnp.int32, (high - low, 128), 0) + low
            pick = jnp.where(place == table_ref[n : n + 1, :], 1.0, 0.0).astype(BF)
            out_ref[:, n * 128 : (n + 1) * 128] = jnp.dot(
                normed[:, low:high], pick, preferred_element_type=F32
            ).astype(BF)

    return pl.pallas_call(
        body,
        out_shape=jax.ShapeDtypeStruct((rows, width), BF),
        in_specs=[SMEM, ANY, VMEM, VMEM],
        out_specs=VMEM,
        scratch_shapes=[
            pltpu.VMEM((MT, tile_len, width), BF),
            pltpu.VMEM((rows, width), BF),
            pltpu.SemaphoreType.DMA((MT,)),
        ],
        name="hold_and_norm",
    )(source, recv, gain.reshape(1, width), table)


def conv_scores(canvas, top, bottom, left, right, weight, bias, readout):
    height, breadth, channels = canvas.shape
    hidden = weight.shape[1]
    step = 8
    pixels = step * breadth

    def side(edge):
        return jnp.concatenate([edge[0:height], edge[1 : height + 1], edge[2 : height + 2]], axis=1)

    def body(canvas_ref, top_ref, bottom_ref, left_ref, right_ref, w_ref, bias_ref, read_ref, out_ref,
             padded, lside, rside, sem):
        i = pl.program_id(0)

        def w_of(col):
            return jnp.concatenate(
                [w_ref[(row * 3 + col) * channels : (row * 3 + col + 1) * channels, :] for row in range(3)],
                axis=0,
            )

        @pl.when(i == 0)
        def _():
            fetch = pltpu.make_async_copy(canvas_ref, padded.at[pl.ds(1, height)], sem)
            fetch.start()
            padded[0:1] = top_ref[...]
            padded[height + 1 : height + 2] = bottom_ref[...]
            sides = (height // step, step, hidden)
            lside[...] = jnp.dot(left_ref[...], w_of(0), preferred_element_type=F32).reshape(sides)
            rside[...] = jnp.dot(right_ref[...], w_of(2), preferred_element_type=F32).reshape(sides)
            fetch.wait()

        window = jnp.concatenate(
            [padded[pl.ds(i * step + row, step)].reshape(pixels, channels) for row in range(3)], axis=1
        )
        before = jnp.dot(window, w_of(0), preferred_element_type=F32)
        at = jnp.dot(window, w_of(1), preferred_element_type=F32)
        after = jnp.dot(window, w_of(2), preferred_element_type=F32)
        before = pltpu.roll(before, 1, 0).reshape(step, breadth, hidden)
        after = pltpu.roll(after, pixels - 1, 0).reshape(step, breadth, hidden)
        col = lax.broadcasted_iota(jnp.int32, (step, breadth, hidden), 1)
        lrow = lside[i]
        rrow = rside[i]
        before = jnp.where(col == 0, lrow[:, None, :], before)
        after = jnp.where(col == breadth - 1, rrow[:, None, :], after)
        x = (before + after).reshape(pixels, hidden) + at + bias_ref[...]
        inner = math.sqrt(2.0 / math.pi) * (x + 0.044715 * (x * x * x))
        h = x * (0.5 * (1.0 + jnp.tanh(inner)))
        h = h * read_ref[...]
        half = h[:, 0:128]
        for k in range(1, hidden // 128):
            half = half + h[:, k * 128 : (k + 1) * 128]
        ones = jnp.ones((8, 128), F32)
        score = lax.dot_general(
            ones, half, (((1,), (1,)), ((), ())), precision=lax.Precision.HIGHEST, preferred_element_type=F32
        )
        for r in range(step):
            out_ref[0, r : r + 1, :] = score[0:1, r * breadth : (r + 1) * breadth]

    out = pl.pallas_call(
        body,
        grid=(height // step,),
        out_shape=jax.ShapeDtypeStruct((height // step, step, breadth), F32),
        in_specs=[ANY] + [pl.BlockSpec(memory_space=pltpu.VMEM)] * 7,
        out_specs=pl.BlockSpec((1, step, breadth), lambda i: (i, 0, 0)),
        scratch_shapes=[
            pltpu.VMEM((height + 2, breadth, channels), BF),
            pltpu.VMEM((height // step, step, hidden), F32),
            pltpu.VMEM((height // step, step, hidden), F32),
            pltpu.SemaphoreType.DMA,
        ],
        compiler_params=pltpu.CompilerParams(vmem_limit_bytes=32 << 20),
        name="conv_scores",
    )(canvas, top, bottom, side(left), side(right), weight, bias.reshape(1, hidden), readout.reshape(1, hidden))
    return out.reshape(height, breadth)


def pack_rows(weight):
    rows, cols = weight.shape
    eights, tiles = rows // 8, cols // 128
    spare = -(-tiles // 8)
    ahead = eights * tiles

    def body(w_ref, out_ref):
        w = w_ref[...].astype(F32)
        zero = jnp.zeros((1, 128), F32)
        for j in range(spare):
            pieces = [
                w[rows - 1 : rows, t * 128 : (t + 1) * 128] if t < tiles else zero
                for t in range(8 * j, 8 * j + 8)
            ]
            out_ref[:, (ahead + j) * 128 : (ahead + j + 1) * 128] = jnp.concatenate(pieces, axis=0).astype(BF)
        for h in range(HEADS):
            for b in range(eights):
                for kind in range(3):
                    at, low = (3 * (eights * h + b) + kind) * 128, (kind * HEADS + h) * 128
                    out_ref[:, at : at + 128] = w[8 * b : 8 * b + 8, low : low + 128].astype(BF)

    return pl.pallas_call(
        body,
        out_shape=jax.ShapeDtypeStruct((8, spare * 128 + eights * cols), BF),
        in_specs=[VMEM],
        out_specs=VMEM,
        name="pack_rows",
    )(weight)


def project_and_attend(near_tokens, bias, packed, sharp):
    near, width = near_tokens.shape
    rows = near // 3
    deep = packed.shape[0]
    eights, parts = width // deep, deep // 8
    spare = -(-3 * HEADS // 8)
    scale = 1.0 / math.sqrt(HD)

    def body(x, bias, w_ref, *refs):
        ext = refs[:spare]
        sharp_ref, out_ref, wide, lasts, q_buf, k_buf, v_buf = refs[spare:]
        n = pl.program_id(0)
        head = jnp.minimum(n, HEADS - 1)

        @pl.when(n == 0)
        def _():
            for j in range(spare):
                wide[j] = ext[j][...].astype(F32)
            for j in range(spare):
                for s in range(8):
                    lasts[8 * j + s] = wide[j, pl.ds(s, parts, stride=8), :].astype(BF)
            q_buf[1] = jnp.zeros((rows, HD), BF)
            k_buf[1] = jnp.zeros((near, HD), BF)
            v_buf[1] = jnp.zeros((near, HD), BF)

        done = (n + 1) % 2
        logits = lax.dot_general(
            q_buf[done], k_buf[done], (((1,), (1,)), ((), ())), preferred_element_type=F32
        )
        logits = logits * scale + bias[...]
        peak = jnp.max(logits, axis=1, keepdims=True)
        weights = jnp.exp(logits - peak)
        total = jnp.sum(weights, axis=1, keepdims=True)
        result = jnp.dot(weights.astype(BF), v_buf[done], preferred_element_type=F32)
        out_ref[...] = (result / total).astype(BF)

        q = jnp.zeros((rows, HD), F32)
        kv = jnp.zeros((near, 2 * HD), F32)
        for b in range(eights):
            at = b * deep
            q = q + jnp.dot(
                x[rows : 2 * rows, at : at + deep], w_ref[:, 3 * b * HD : (3 * b + 1) * HD], preferred_element_type=F32
            )
            both = w_ref[:, (3 * b + 1) * HD : (3 * b + 3) * HD]
            kv = kv + jnp.dot(x[:, at : at + deep], both, preferred_element_type=F32)
        at = eights * deep
        q = q + jnp.dot(x[rows : 2 * rows, at:], lasts[head], preferred_element_type=F32)
        both = jnp.concatenate([lasts[head + HEADS], lasts[head + 2 * HEADS]], axis=1)
        kv = kv + jnp.dot(x[:, at:], both, preferred_element_type=F32)
        new = n % 2
        q_buf[new] = q.astype(BF)
        k_buf[new] = (kv[:, :HD] * sharp_ref[...]).astype(BF)
        v_buf[new] = kv[:, HD:].astype(BF)

    def ext_spec(j):
        return pl.BlockSpec((deep, 128), lambda n: (0, 3 * eights * HEADS + j))

    return pl.pallas_call(
        body,
        grid=(HEADS + 1,),
        out_shape=jax.ShapeDtypeStruct((rows, HW), BF),
        in_specs=[VMEM, VMEM, pl.BlockSpec((deep, 3 * eights * HD), lambda n: (0, jnp.minimum(n, HEADS - 1)))]
        + [ext_spec(j) for j in range(spare)]
        + [VMEM],
        out_specs=pl.BlockSpec((rows, HD), lambda n: (0, jnp.maximum(n - 1, 0))),
        scratch_shapes=[
            pltpu.VMEM((spare, deep, 128), F32),
            pltpu.VMEM((8 * spare, parts, HD), BF),
            pltpu.VMEM((2, rows, HD), BF),
            pltpu.VMEM((2, near, HD), BF),
            pltpu.VMEM((2, near, HD), BF),
        ],
        compiler_params=pltpu.CompilerParams(vmem_limit_bytes=48 << 20),
        name="project_and_attend",
    )(near_tokens, bias, *([packed] * (1 + spare)), sharp)


def shards(
    canvas,
    conv_weight,
    conv_bias,
    score_weight,
    tile_tokens,
    tile_cell,
    tile_count,
    holder_order,
    tile_image,
    ln_gain,
    qkv_weight,
):
    axes = ("grp", "dev")
    holders = lax.axis_size("dev")
    parts = holders * lax.axis_size("grp")
    own = lax.axis_index("dev")
    counts, order = tile_count[0], holder_order[0]
    tile_len = tile_tokens.shape[1]
    held_rows = MT * tile_len

    sent = send_order(counts, order, own.reshape(1), tile_tokens)
    recv = lax.all_to_all(sent, "dev", split_axis=0, concat_axis=0, tiled=True)

    packed = lax.all_gather(pack_rows(qkv_weight), axes, axis=0, tiled=True)

    up, down = ring_pairs("grp")
    top = lax.ppermute(canvas[-1:], "grp", up)
    bottom = lax.ppermute(canvas[:1], "grp", down)
    up, down = ring_pairs("dev")

    def edge(col):
        return jnp.concatenate([top[:, col], canvas[:, col], bottom[:, col]], axis=0)

    left = lax.ppermute(edge(-1), "dev", up)
    right = lax.ppermute(edge(0), "dev", down)
    score_map = conv_scores(canvas, top, bottom, left, right, conv_weight, conv_bias, score_weight)

    ranks = jnp.arange(holders, dtype=jnp.int32)
    first = jnp.sum(jnp.where(ranks < own, counts, 0))
    place_of = jnp.sum(jnp.where(order[None, :] == ranks[:, None], ranks[None, :], 0), axis=1)
    slot_for = (place_of - first) & (holders - 1)
    cells = jnp.take(tile_cell[0], slot_for)
    send_score = jnp.take(score_map.reshape(-1), cells).astype(BF)
    send_score = jnp.stack([jnp.roll(send_score, 1), send_score, jnp.roll(send_score, -1)], axis=1)
    _, send_score = lax.optimization_barrier((recv, send_score))
    recv_score = lax.all_to_all(send_score, "dev", split_axis=0, concat_axis=0, tiled=True)

    near_holders = jnp.clip(own + jnp.arange(-1, 2, dtype=jnp.int32), 0, holders - 1)
    places = jnp.sum(jnp.where(order[None, :] == near_holders[:, None], ranks[None, :], 0), axis=1)
    wanted = jnp.arange(MT, dtype=jnp.int32)[None, :] * holders + places[:, None]
    ends = jnp.sum(jnp.where(ranks[None, :] <= ranks[:, None], counts[None, :], 0), axis=1)
    source = jnp.sum((ends <= wanted[:, :, None]).astype(jnp.int32), axis=2)
    picked = source[:, :, None] == ranks
    near_score = jnp.sum(jnp.where(picked, recv_score.astype(F32).T[:, None, :], 0.0), axis=2)
    sharp = jnp.repeat(0.5 + jax.nn.softplus(near_score.reshape(-1)), tile_len)[:, None]

    here = hold_and_norm(source[1], recv, ln_gain, parts)
    before = lax.ppermute(here, "dev", up)
    after = lax.ppermute(here, "dev", down)

    all_ids = tile_image[0]
    places = own * MT - MT + jnp.arange(3 * MT, dtype=jnp.int32)
    inside = (places >= 0) & (places < all_ids.shape[0])
    near_ids = jnp.where(inside, jnp.take(all_ids, jnp.clip(places, 0, all_ids.shape[0] - 1)), -1)
    key_ids = jnp.repeat(near_ids, tile_len)
    own_ids = key_ids[held_rows : 2 * held_rows]
    near_tokens = jnp.concatenate([before, here, after], axis=0)
    bias = jnp.where(own_ids[:, None] == key_ids[None, :], 0.0, -1e30)
    attended = project_and_attend(near_tokens, bias, packed, sharp)
    return (score_map, attended)


def solution(mesh):
    placed = (
        P("grp", "dev", None),
        P(),
        P(),
        P(),
        P(("grp", "dev"), None, None),
        P("grp", "dev"),
        P("grp", None),
        P("grp", None),
        P("grp", None),
        P(),
        P(("grp", "dev"), None),
    )
    return jax.shard_map(
        shards,
        mesh=mesh,
        in_specs=placed,
        out_specs=(P("grp", "dev"), P(("grp", "dev"), None)),
        check_vma=False,
    )
```

```python
import math

import jax
import jax.numpy as jnp
import numpy as np
from jax import lax
from jax.experimental import pallas as pl
from jax.experimental.pallas import tpu as pltpu
from jax.sharding import PartitionSpec as P


HD = 128
HEADS = 13
HW = HEADS * HD
MT = 8
BF = jnp.bfloat16
F32 = jnp.float32
ANY = pl.BlockSpec(memory_space=pl.ANY)
SMEM = pl.BlockSpec(memory_space=pltpu.SMEM)
VMEM = pl.BlockSpec(memory_space=pltpu.VMEM)


def ring_pairs(axis):
    size = lax.axis_size(axis)
    up = [(i, i + 1) for i in range(size - 1)]
    return up, [(j, i) for i, j in up]


def send_order(counts, order, own, tokens):
    holders = order.shape[0]

    def body(counts_ref, order_ref, own_ref, tok_ref, out_ref, tiles, in_sems, out_sems):
        fetch = [pltpu.make_async_copy(tok_ref.at[s], tiles.at[s], in_sems.at[s]) for s in range(holders)]
        for c in fetch:
            c.start()
        first = lax.fori_loop(0, own_ref[0], lambda j, acc: acc + counts_ref[j], jnp.int32(0))

        def copy(s):
            holder = order_ref[(first + s) & (holders - 1)]
            return pltpu.make_async_copy(tiles.at[s], out_ref.at[holder], out_sems.at[s])

        for s in range(holders):
            fetch[s].wait()
            copy(s).start()
        for s in range(holders):
            copy(s).wait()

    return pl.pallas_call(
        body,
        out_shape=jax.ShapeDtypeStruct(tokens.shape, tokens.dtype),
        in_specs=[SMEM, SMEM, SMEM, ANY],
        out_specs=ANY,
        scratch_shapes=[
            pltpu.VMEM(tokens.shape, tokens.dtype),
            pltpu.SemaphoreType.DMA((holders,)),
            pltpu.SemaphoreType.DMA((holders,)),
        ],
        name="send_order",
    )(counts, order, own, tokens)


def spread_index(parts, rows):
    part, row = np.arange(parts)[:, None], np.arange(8)[None, :]
    main = [(rows * part + 8 * b + row).reshape(-1) for b in range(rows // 8)]
    return np.concatenate(main + [rows * np.arange(parts) + rows - 1]).astype(np.int32)


def hold_and_norm(source, recv, gain, parts):
    tile_len, width = recv.shape[1], recv.shape[2]
    rows = MT * tile_len
    index = spread_index(parts, width // parts)
    blocks = width // 128
    table = jnp.asarray(index.reshape(blocks, 128))

    def body(src_ref, recv_ref, gain_ref, table_ref, out_ref, tiles, normed, sems):
        copies = [
            pltpu.make_async_copy(recv_ref.at[src_ref[m]], tiles.at[m], sems.at[m]) for m in range(MT)
        ]
        for c in copies:
            c.start()
        for m in range(MT):
            copies[m].wait()
            values = tiles[m].astype(F32)
            center = jnp.mean(values, axis=1, keepdims=True)
            values = values - center
            spread = jnp.mean(values * values, axis=1, keepdims=True)
            scaled = values * lax.rsqrt(spread + 1e-06) * gain_ref[...]
            normed[m * tile_len : (m + 1) * tile_len, :] = scaled.astype(BF)
        for n in range(blocks):
            part = index[n * 128 : (n + 1) * 128]
            low = int(part.min()) // 128 * 128
            high = int(part.max()) // 128 * 128 + 128
            place = lax.broadcasted_iota(jnp.int32, (high - low, 128), 0) + low
            pick = jnp.where(place == table_ref[n : n + 1, :], 1.0, 0.0).astype(BF)
            out_ref[:, n * 128 : (n + 1) * 128] = jnp.dot(
                normed[:, low:high], pick, preferred_element_type=F32
            ).astype(BF)

    return pl.pallas_call(
        body,
        out_shape=jax.ShapeDtypeStruct((rows, width), BF),
        in_specs=[SMEM, ANY, VMEM, VMEM],
        out_specs=VMEM,
        scratch_shapes=[
            pltpu.VMEM((MT, tile_len, width), BF),
            pltpu.VMEM((rows, width), BF),
            pltpu.SemaphoreType.DMA((MT,)),
        ],
        name="hold_and_norm",
    )(source, recv, gain.reshape(1, width), table)


def conv_scores(canvas, top, bottom, left, right, weight, bias, readout):
    height, breadth, channels = canvas.shape
    hidden = weight.shape[1]
    step = 8
    pixels = step * breadth

    def side(edge):
        return jnp.concatenate([edge[0:height], edge[1 : height + 1], edge[2 : height + 2]], axis=1)

    def body(canvas_ref, top_ref, bottom_ref, left_ref, right_ref, w_ref, bias_ref, read_ref, out_ref,
             padded, lside, rside, sem):
        i = pl.program_id(0)

        def w_of(col):
            return jnp.concatenate(
                [w_ref[(row * 3 + col) * channels : (row * 3 + col + 1) * channels, :] for row in range(3)],
                axis=0,
            )

        @pl.when(i == 0)
        def _():
            fetch = pltpu.make_async_copy(canvas_ref, padded.at[pl.ds(1, height)], sem)
            fetch.start()
            padded[0:1] = top_ref[...]
            padded[height + 1 : height + 2] = bottom_ref[...]
            sides = (height // step, step, hidden)
            lside[...] = jnp.dot(left_ref[...], w_of(0), preferred_element_type=F32).reshape(sides)
            rside[...] = jnp.dot(right_ref[...], w_of(2), preferred_element_type=F32).reshape(sides)
            fetch.wait()

        window = jnp.concatenate(
            [padded[pl.ds(i * step + row, step)].reshape(pixels, channels) for row in range(3)], axis=1
        )
        before = jnp.dot(window, w_of(0), preferred_element_type=F32)
        at = jnp.dot(window, w_of(1), preferred_element_type=F32)
        after = jnp.dot(window, w_of(2), preferred_element_type=F32)
        before = pltpu.roll(before, 1, 0).reshape(step, breadth, hidden)
        after = pltpu.roll(after, pixels - 1, 0).reshape(step, breadth, hidden)
        col = lax.broadcasted_iota(jnp.int32, (step, breadth, hidden), 1)
        lrow = lside[i]
        rrow = rside[i]
        before = jnp.where(col == 0, lrow[:, None, :], before)
        after = jnp.where(col == breadth - 1, rrow[:, None, :], after)
        x = (before + after).reshape(pixels, hidden) + at + bias_ref[...]
        inner = math.sqrt(2.0 / math.pi) * (x + 0.044715 * (x * x * x))
        h = x * (0.5 * (1.0 + jnp.tanh(inner)))
        h = h * read_ref[...]
        half = h[:, 0:128]
        for k in range(1, hidden // 128):
            half = half + h[:, k * 128 : (k + 1) * 128]
        ones = jnp.ones((8, 128), F32)
        score = lax.dot_general(
            ones, half, (((1,), (1,)), ((), ())), precision=lax.Precision.HIGHEST, preferred_element_type=F32
        )
        for r in range(step):
            out_ref[0, r : r + 1, :] = score[0:1, r * breadth : (r + 1) * breadth]

    out = pl.pallas_call(
        body,
        grid=(height // step,),
        out_shape=jax.ShapeDtypeStruct((height // step, step, breadth), F32),
        in_specs=[ANY] + [pl.BlockSpec(memory_space=pltpu.VMEM)] * 7,
        out_specs=pl.BlockSpec((1, step, breadth), lambda i: (i, 0, 0)),
        scratch_shapes=[
            pltpu.VMEM((height + 2, breadth, channels), BF),
            pltpu.VMEM((height // step, step, hidden), F32),
            pltpu.VMEM((height // step, step, hidden), F32),
            pltpu.SemaphoreType.DMA,
        ],
        compiler_params=pltpu.CompilerParams(vmem_limit_bytes=32 << 20),
        name="conv_scores",
    )(canvas, top, bottom, side(left), side(right), weight, bias.reshape(1, hidden), readout.reshape(1, hidden))
    return out.reshape(height, breadth)


def pack_rows(weight):
    rows, cols = weight.shape
    eights, tiles = rows // 8, cols // 128
    spare = -(-tiles // 8)
    ahead = eights * tiles

    def body(w_ref, out_ref):
        w = w_ref[...].astype(F32)
        zero = jnp.zeros((1, 128), F32)
        for j in range(spare):
            pieces = [
                w[rows - 1 : rows, t * 128 : (t + 1) * 128] if t < tiles else zero
                for t in range(8 * j, 8 * j + 8)
            ]
            out_ref[:, (ahead + j) * 128 : (ahead + j + 1) * 128] = jnp.concatenate(pieces, axis=0).astype(BF)
        for h in range(HEADS):
            for b in range(eights):
                for kind in range(3):
                    at, low = (3 * (eights * h + b) + kind) * 128, (kind * HEADS + h) * 128
                    out_ref[:, at : at + 128] = w[8 * b : 8 * b + 8, low : low + 128].astype(BF)

    return pl.pallas_call(
        body,
        out_shape=jax.ShapeDtypeStruct((8, spare * 128 + eights * cols), BF),
        in_specs=[VMEM],
        out_specs=VMEM,
        name="pack_rows",
    )(weight)


def project_and_attend(before, here, after, bias, packed, sharp):
    rows, width = here.shape
    near = 3 * rows
    deep = packed.shape[0]
    eights, parts = width // deep, deep // 8
    spare = -(-3 * HEADS // 8)
    scale = 1.0 / math.sqrt(HD)

    def body(xb, xh, xa, bias, w_ref, *refs):
        ext = refs[:spare]
        sharp_ref, out_ref, x, wide, lasts, q_buf, k_buf, v_buf = refs[spare:]
        n = pl.program_id(0)
        head = jnp.minimum(n, HEADS - 1)

        @pl.when(n == 0)
        def _():
            x[0:rows] = xb[...]
            x[rows : 2 * rows] = xh[...]
            x[2 * rows :] = xa[...]
            for j in range(spare):
                wide[j] = ext[j][...].astype(F32)
            for j in range(spare):
                for s in range(8):
                    lasts[8 * j + s] = wide[j, pl.ds(s, parts, stride=8), :].astype(BF)
            q_buf[1] = jnp.zeros((rows, HD), BF)
            k_buf[1] = jnp.zeros((near, HD), BF)
            v_buf[1] = jnp.zeros((near, HD), BF)

        done = (n + 1) % 2
        logits = lax.dot_general(
            q_buf[done], k_buf[done], (((1,), (1,)), ((), ())), preferred_element_type=F32
        )
        logits = logits * scale + bias[...]
        peak = jnp.max(logits, axis=1, keepdims=True)
        weights = jnp.exp(logits - peak)
        total = jnp.sum(weights, axis=1, keepdims=True)
        result = jnp.dot(weights.astype(BF), v_buf[done], preferred_element_type=F32)
        out_ref[...] = (result / total).astype(BF)

        q = jnp.zeros((rows, HD), F32)
        kv = jnp.zeros((near, 2 * HD), F32)
        for b in range(eights):
            at = b * deep
            q = q + jnp.dot(
                x[rows : 2 * rows, at : at + deep], w_ref[:, 3 * b * HD : (3 * b + 1) * HD], preferred_element_type=F32
            )
            both = w_ref[:, (3 * b + 1) * HD : (3 * b + 3) * HD]
            kv = kv + jnp.dot(x[:, at : at + deep], both, preferred_element_type=F32)
        at = eights * deep
        q = q + jnp.dot(x[rows : 2 * rows, at:], lasts[head], preferred_element_type=F32)
        both = jnp.concatenate([lasts[head + HEADS], lasts[head + 2 * HEADS]], axis=1)
        kv = kv + jnp.dot(x[:, at:], both, preferred_element_type=F32)
        new = n % 2
        q_buf[new] = q.astype(BF)
        k_buf[new] = (kv[:, :HD] * sharp_ref[...]).astype(BF)
        v_buf[new] = kv[:, HD:].astype(BF)

    def ext_spec(j):
        return pl.BlockSpec((deep, 128), lambda n: (0, 3 * eights * HEADS + j))

    return pl.pallas_call(
        body,
        grid=(HEADS + 1,),
        out_shape=jax.ShapeDtypeStruct((rows, HW), BF),
        in_specs=[VMEM, VMEM, VMEM, VMEM, pl.BlockSpec((deep, 3 * eights * HD), lambda n: (0, jnp.minimum(n, HEADS - 1)))]
        + [ext_spec(j) for j in range(spare)]
        + [VMEM],
        out_specs=pl.BlockSpec((rows, HD), lambda n: (0, jnp.maximum(n - 1, 0))),
        scratch_shapes=[
            pltpu.VMEM((near, width), BF),
            pltpu.VMEM((spare, deep, 128), F32),
            pltpu.VMEM((8 * spare, parts, HD), BF),
            pltpu.VMEM((2, rows, HD), BF),
            pltpu.VMEM((2, near, HD), BF),
            pltpu.VMEM((2, near, HD), BF),
        ],
        compiler_params=pltpu.CompilerParams(vmem_limit_bytes=48 << 20),
        name="project_and_attend",
    )(before, here, after, bias, *([packed] * (1 + spare)), sharp)


def shards(
    canvas,
    conv_weight,
    conv_bias,
    score_weight,
    tile_tokens,
    tile_cell,
    tile_count,
    holder_order,
    tile_image,
    ln_gain,
    qkv_weight,
):
    axes = ("grp", "dev")
    holders = lax.axis_size("dev")
    parts = holders * lax.axis_size("grp")
    own = lax.axis_index("dev")
    counts, order = tile_count[0], holder_order[0]
    tile_len = tile_tokens.shape[1]
    held_rows = MT * tile_len

    sent = send_order(counts, order, own.reshape(1), tile_tokens)
    recv = lax.all_to_all(sent, "dev", split_axis=0, concat_axis=0, tiled=True)

    packed = lax.all_gather(pack_rows(qkv_weight), axes, axis=0, tiled=True)

    up, down = ring_pairs("grp")
    top = lax.ppermute(canvas[-1:], "grp", up)
    bottom = lax.ppermute(canvas[:1], "grp", down)
    up, down = ring_pairs("dev")

    def edge(col):
        return jnp.concatenate([top[:, col], canvas[:, col], bottom[:, col]], axis=0)

    left = lax.ppermute(edge(-1), "dev", up)
    right = lax.ppermute(edge(0), "dev", down)
    score_map = conv_scores(canvas, top, bottom, left, right, conv_weight, conv_bias, score_weight)

    ranks = jnp.arange(holders, dtype=jnp.int32)
    first = jnp.sum(jnp.where(ranks < own, counts, 0))
    place_of = jnp.sum(jnp.where(order[None, :] == ranks[:, None], ranks[None, :], 0), axis=1)
    slot_for = (place_of - first) & (holders - 1)
    cells = jnp.take(tile_cell[0], slot_for)
    send_score = jnp.take(score_map.reshape(-1), cells).astype(BF)
    send_score = jnp.stack([jnp.roll(send_score, 1), send_score, jnp.roll(send_score, -1)], axis=1)
    _, send_score = lax.optimization_barrier((recv, send_score))
    recv_score = lax.all_to_all(send_score, "dev", split_axis=0, concat_axis=0, tiled=True)

    near_holders = jnp.clip(own + jnp.arange(-1, 2, dtype=jnp.int32), 0, holders - 1)
    places = jnp.sum(jnp.where(order[None, :] == near_holders[:, None], ranks[None, :], 0), axis=1)
    wanted = jnp.arange(MT, dtype=jnp.int32)[None, :] * holders + places[:, None]
    ends = jnp.sum(jnp.where(ranks[None, :] <= ranks[:, None], counts[None, :], 0), axis=1)
    source = jnp.sum((ends <= wanted[:, :, None]).astype(jnp.int32), axis=2)
    picked = source[:, :, None] == ranks
    near_score = jnp.sum(jnp.where(picked, recv_score.astype(F32).T[:, None, :], 0.0), axis=2)
    sharp = jnp.repeat(0.5 + jax.nn.softplus(near_score.reshape(-1)), tile_len)[:, None]

    here = hold_and_norm(source[1], recv, ln_gain, parts)
    before = lax.ppermute(here, "dev", up)
    after = lax.ppermute(here, "dev", down)

    all_ids = tile_image[0]
    places = own * MT - MT + jnp.arange(3 * MT, dtype=jnp.int32)
    inside = (places >= 0) & (places < all_ids.shape[0])
    near_ids = jnp.where(inside, jnp.take(all_ids, jnp.clip(places, 0, all_ids.shape[0] - 1)), -1)
    key_ids = jnp.repeat(near_ids, tile_len)
    own_ids = key_ids[held_rows : 2 * held_rows]
    bias = jnp.where(own_ids[:, None] == key_ids[None, :], 0.0, -1e30)
    attended = project_and_attend(before, here, after, bias, packed, sharp)
    return (score_map, attended)


def solution(mesh):
    placed = (
        P("grp", "dev", None),
        P(),
        P(),
        P(),
        P(("grp", "dev"), None, None),
        P("grp", "dev"),
        P("grp", None),
        P("grp", None),
        P("grp", None),
        P(),
        P(("grp", "dev"), None),
    )
    return jax.shard_map(
        shards,
        mesh=mesh,
        in_specs=placed,
        out_specs=(P("grp", "dev"), P(("grp", "dev"), None)),
        check_vma=False,
    )
```
